256 devices in a mesh: frame: 16 (over z_lo, x), strip: 16 (over z_hi, y, core).
Axes of the slice: x: 4, y: 4, z: 8 (z_hi: 2, z_lo: 4; z = z_hi * 4 + z_lo), core: 2. Of those that a mesh axis runs over, the one named last changes fastest.
Arguments:
- movie: bfloat16 [128, 1024, 2048], P('frame', 'strip'), may hold values from -17 to 22, as said below
Outputs:
- lag_maps: float32 [25, 1024, 2048], P(None, 'strip', 'frame')
The draws below stay inside these ranges and needn't reach their ends.
Inputs may be any that keep to these rules, and one draw needn't show every extreme that they name: Frames of a camera movie.
All inputs are finite; a program needn't handle non-finite values.
Results may differ from the reference program's by a relative error of at most 0.0004.
Values may be sent and summed in bfloat16 or wider, within the bound.
A program may use at most 64 MiB of HBM per device.

```python
import math
import jax
import jax.numpy as jnp
from jax import lax

FR_DEV = 8
WIDTH = 2048
LAGS = 25
FRAMES = 128
HEIGHT = 1024
N_FRAME = 16


def draw_movie(key, part):
    key_offset = jax.random.fold_in(key, 11)
    key_scale = jax.random.fold_in(key, 12)
    key_noise = jax.random.fold_in(key, 13)
    offset = jnp.exp(jax.random.uniform(key_offset, (HEIGHT, WIDTH), jnp.float32, 0.0, math.log(4.0)))
    pixel_scale = jnp.exp(jax.random.uniform(key_scale, (HEIGHT, WIDTH), jnp.float32, -math.log(2.0), math.log(2.0)))
    noise_field = jnp.clip(jax.random.normal(key_noise, (FRAMES, HEIGHT, WIDTH), jnp.float32), -4.0, 4.0)
    blurred = noise_field + 0.6 * jnp.roll(noise_field, 1, axis=1) + 0.6 * jnp.roll(noise_field, 1, axis=2)
    return (offset + pixel_scale * blurred).astype(jnp.bfloat16)


def setup_inputs(seed: int = 0) -> dict:
    key_of = jax.random.split(jax.random.key(seed), 2)
    movie = draw_movie(jax.random.fold_in(key_of[1], 71), 0)
    return {"movie": movie}


def reference(movie):
    frame_blocks = movie.reshape(N_FRAME, FR_DEV, HEIGHT, WIDTH)

    def add_sum(running, movie_block):
        return running + jnp.sum(movie_block.astype(jnp.float32), axis=0), None

    running, _ = lax.scan(add_sum, jnp.zeros((HEIGHT, WIDTH), jnp.float32), frame_blocks)
    pixel_mean = running / FRAMES

    def add_lags(lag_total, movie_block):
        fluctuation = movie_block.astype(jnp.float32) - pixel_mean
        padded = jnp.pad(fluctuation, ((0, 0), (2, 2), (2, 2)))
        centre = padded[:, 2:2 + HEIGHT, 2:2 + WIDTH]
        products = []
        for row_lag in range(-2, 3):
            for col_lag in range(-2, 3):
                shifted = padded[:, 2 + row_lag:2 + row_lag + HEIGHT, 2 + col_lag:2 + col_lag + WIDTH]
                products.append(jnp.sum(centre * shifted, axis=0))
        return lag_total + jnp.stack(products), None

    lag_total, _ = lax.scan(add_lags, jnp.zeros((LAGS, HEIGHT, WIDTH), jnp.float32), frame_blocks)
    return lag_total / FRAMES
```

```python
import functools

import jax
import jax.numpy as jnp
from jax import lax
from jax.experimental import pallas as pl
from jax.experimental.pallas import tpu as pltpu
from jax.sharding import PartitionSpec as P

MESH = pl.DeviceIdType.MESH
LANES = 128
CH = 8
REACH = 2
F32 = jnp.float32
BF16 = jnp.bfloat16


def lag_kernel(
    n_frame, n_strip, n_z, frames_total,
    movie, out, block, edges_in, edges_out, rows_in, rows_out, held, spread, picked, work,
    send_sem, recv_sem, own_sem, held_sem, edge_send, edge_recv, row_send, row_recv,
):
    frames, rows, width = movie.shape
    chunks = rows // CH
    n_x = n_frame // n_z
    me = lax.axis_index("frame")
    strip = lax.axis_index("strip")
    z, x = me // n_x, lax.rem(me, n_x)
    inverse = 1.0 / frames_total

    lane = lax.broadcasted_iota(jnp.int32, (8, LANES), 1)
    has_left, has_right = me > 0, me < n_frame - 1

    def peer(k):
        dx, dz = k // n_z, lax.rem(k, n_z)
        return lax.rem(z + dz, n_z) * n_x + lax.rem(x + dx, n_x)

    def chunk_at(step):
        return lax.rem(chunks - step, chunks)

    def columns(g):
        return pl.ds(pl.multiple_of(g * LANES, LANES), LANES)

    def block_copy(c, g, source):
        return pltpu.make_async_remote_copy(
            src_ref=movie.at[:, pl.ds(pl.multiple_of(c * CH, CH), CH), columns(g)],
            dst_ref=block.at[c, source],
            send_sem=send_sem.at[c, g], recv_sem=recv_sem.at[c, source],
            device_id={"frame": g}, device_id_type=MESH,
        )

    def own_copy(c):
        return pltpu.make_async_copy(
            movie.at[:, pl.ds(pl.multiple_of(c * CH, CH), CH), columns(me)],
            block.at[c, me], own_sem.at[c],
        )

    def edge_copy(g, source):
        return pltpu.make_async_remote_copy(
            src_ref=edges_out.at[g], dst_ref=edges_in.at[source],
            send_sem=edge_send.at[g], recv_sem=edge_recv.at[source],
            device_id={"frame": g}, device_id_type=MESH,
        )

    def row_copy(side, to):
        return pltpu.make_async_remote_copy(
            src_ref=rows_out.at[side], dst_ref=rows_in.at[side],
            send_sem=row_send.at[side], recv_sem=row_recv.at[side],
            device_id={"strip": to}, device_id_type=MESH,
        )

    above, below = jnp.maximum(strip - 1, 0), jnp.minimum(strip + 1, n_strip - 1)
    has_above, has_below = strip > 0, strip < n_strip - 1

    whole = pltpu.make_async_copy(movie, held, held_sem)
    whole.start()

    @pl.loop(0, chunks)
    def _(c):
        own_copy(c).start()

    barrier = pltpu.get_barrier_semaphore()

    @pl.loop(1, n_frame)
    def _(k):
        pl.semaphore_signal(barrier, inc=1, device_id={"frame": peer(k)}, device_id_type=MESH)

    @pl.when(has_above)
    def _():
        pl.semaphore_signal(barrier, inc=1, device_id={"strip": above}, device_id_type=MESH)

    @pl.when(has_below)
    def _():
        pl.semaphore_signal(barrier, inc=1, device_id={"strip": below}, device_id_type=MESH)

    neighbours = jnp.where(has_above, 1, 0) + jnp.where(has_below, 1, 0)
    pl.semaphore_wait(barrier, n_frame - 1 + neighbours)

    @pl.loop(0, chunks)
    def _(step):
        @pl.loop(1, n_frame)
        def _(k):
            block_copy(chunk_at(step), peer(k), me).start()

    whole.wait()
    pick_row = lax.broadcasted_iota(jnp.int32, (width, LANES), 0)
    pick_lane = lax.broadcasted_iota(jnp.int32, (width, LANES), 1)
    j = lax.rem(pick_lane, 4)
    target = (pick_lane // 4) * LANES + jnp.where(j < 2, j - 2, LANES - 2 + j)
    pick = jnp.where((pick_row == target) & (pick_lane < 4 * n_frame), 1.0, 0.0).astype(BF16)
    for f in range(frames):
        picked[pl.ds(f * rows, rows), :] = jnp.dot(held[f], pick, preferred_element_type=F32)

    @pl.loop(0, rows)
    def _(r):
        v = picked[pl.ds(r, frames, stride=rows), :]
        work[pl.ds(pl.multiple_of(r * 8, 8), 8), :] = pltpu.roll(v, 4 * lax.rem(r, 32), 1)

    group = lane // 4

    @pl.loop(0, n_frame)
    def _(g):
        for q in range(rows // 32):
            packed = jnp.zeros((8, LANES), F32)
            for r in range(32):
                v = work[pl.ds((q * 32 + r) * 8, 8), :]
                packed = jnp.where(group == lax.rem(r + g, 32), v, packed)
            edges_out[g, q] = pltpu.roll(packed, lax.rem(LANES - 4 * g, LANES), 1).astype(BF16)

    @pl.loop(1, n_frame)
    def _(k):
        edge_copy(peer(k), me).start()

    edges_in[me] = edges_out[me]

    @pl.loop(1, n_frame)
    def _(k):
        edge_copy(me, peer(k)).wait_recv()

    beside = ((lane >= LANES - 2) & has_left) | ((lane < 2) & has_right)

    def over_frames(total):
        return jnp.sum(total, axis=0, keepdims=True) * inverse

    def prepare(at, row_of, edge_of, edge_total):
        total = row_of(0)
        for i in range(1, n_frame):
            total = total + row_of(i)
        mean, edge_mean = over_frames(total), over_frames(edge_total)
        for i in range(n_frame):
            value = row_of(i) - mean
            edge = jnp.where(beside, edge_of(i) - edge_mean, 0.0)
            spread[at, i, 2] = value
            spread[at, i, 3] = pltpu.roll(jnp.where(lane < 1, edge, value), LANES - 1, 1)
            spread[at, i, 4] = pltpu.roll(jnp.where(lane < 2, edge, value), LANES - 2, 1)
            spread[at, i, 1] = pltpu.roll(jnp.where(lane >= LANES - 1, edge, value), 1, 1)
            spread[at, i, 0] = pltpu.roll(jnp.where(lane >= LANES - 2, edge, value), 2, 1)

    def work_row(i, r):
        return work[pl.ds(i * CH * 8 + r, 8, stride=CH), :]

    def edge_turn(c, r):
        return lax.rem(2 * LANES - 2 - 4 * (lax.rem(c, 32 // CH) * CH + r), LANES)

    def edge_tile(i, c):
        return edges_in[i, c // (32 // CH)].astype(F32)

    def take_chunk(c):
        @pl.loop(1, n_frame)
        def _(k):
            block_copy(c, me, peer(k)).wait_recv()

        own_copy(c).wait()
        for i in range(n_frame):
            work[pl.ds(i * CH * 8, CH * 8), :] = (
                block[c, i].astype(F32).reshape(CH * 8, LANES)
            )

        @pl.loop(0, CH)
        def _(r):
            turn = edge_turn(c, r)
            edge_total = edge_tile(0, c)
            for i in range(1, n_frame):
                edge_total = edge_total + edge_tile(i, c)
            prepare(
                REACH + c * CH + r,
                lambda i: work_row(i, r),
                lambda i: pltpu.roll(edge_tile(i, c), turn, 1),
                pltpu.roll(edge_total, turn, 1),
            )

    def give_rows(side, c, first):
        packed = jnp.zeros((8, LANES), F32)
        for r in range(REACH):
            for i in range(n_frame):
                rows_out[side, r * n_frame + i] = work_row(i, first + r).astype(BF16)
                place = 4 * (r * n_frame + i)
                turn = lax.rem(edge_turn(c, first + r) + 2 + place, LANES)
                packed = jnp.where(
                    group == place // 4, pltpu.roll(edge_tile(i, c), turn, 1), packed
                )
        rows_out[side, REACH * n_frame] = packed.astype(BF16)

    def take_rows(side, base):
        for r in range(REACH):
            packed = rows_in[side, REACH * n_frame].astype(F32)

            def edge_of(i):
                return pltpu.roll(packed, (2 * LANES - 2 - 4 * (r * n_frame + i)) % LANES, 1)

            edge_total = edge_of(0)
            for i in range(1, n_frame):
                edge_total = edge_total + edge_of(i)
            prepare(
                base + r,
                lambda i: rows_in[side, r * n_frame + i].astype(F32),
                edge_of,
                edge_total,
            )

    def lag_row(r):
        def add(i, sums):
            centre = spread[r + REACH, i, REACH]
            return tuple(
                sums[5 * a + b] + centre * spread[r + a, i, b] for a in range(5) for b in range(5)
            )

        sums = lax.fori_loop(
            0, n_frame, add, tuple(jnp.zeros((8, LANES), F32) for _ in range(25)), unroll=4
        )
        for k in range(25):
            out[k, pl.ds(r, 1), :] = over_frames(sums[k])

    def lag_rows(first, last):
        @pl.loop(first, last)
        def _(r):
            lag_row(r)

    take_chunk(0)
    give_rows(0, 0, 0)

    @pl.when(has_above)
    def _():
        row_copy(0, above).start()

    take_chunk(chunks - 1)
    give_rows(1, chunks - 1, CH - REACH)

    @pl.when(has_below)
    def _():
        row_copy(1, below).start()

    lag_rows(REACH, CH - REACH)
    lag_rows(rows - CH + REACH, rows - REACH)

    @pl.loop(2, chunks)
    def _(step):
        c = chunk_at(step)
        take_chunk(c)
        lag_rows(c * CH + REACH, c * CH + CH + REACH)

        @pl.when(step == 2)
        def _():
            zero = jnp.zeros((REACH, n_frame, 5, 8, LANES), F32)

            @pl.when(has_below)
            def _():
                row_copy(0, below).wait_recv()
                take_rows(0, rows + REACH)

            @pl.when(jnp.logical_not(has_below))
            def _():
                spread[rows + REACH : rows + 2 * REACH] = zero

            @pl.when(has_above)
            def _():
                row_copy(1, above).wait_recv()
                take_rows(1, 0)

            @pl.when(jnp.logical_not(has_above))
            def _():
                spread[0:REACH] = zero

            lag_rows(0, REACH)
            lag_rows(rows - REACH, rows)

    lag_rows(CH - REACH, CH + REACH)

    @pl.loop(0, chunks)
    def _(c):
        @pl.loop(1, n_frame)
        def _(k):
            block_copy(c, peer(k), me).wait_send()

    @pl.loop(1, n_frame)
    def _(k):
        edge_copy(peer(k), me).wait_send()

    @pl.when(has_above)
    def _():
        row_copy(0, above).wait_send()

    @pl.when(has_below)
    def _():
        row_copy(1, below).wait_send()


def body(movie):
    frames, rows, width = movie.shape
    n_frame, n_strip = lax.axis_size("frame"), lax.axis_size("strip")
    chunks = rows // CH
    kernel = functools.partial(lag_kernel, n_frame, n_strip, 4, frames * n_frame)
    DMA = pltpu.SemaphoreType.DMA
    return pl.pallas_call(
        kernel,
        out_shape=jax.ShapeDtypeStruct((25, rows, width // n_frame), F32),
        in_specs=[pl.BlockSpec(memory_space=pl.ANY)],
        out_specs=pl.BlockSpec(memory_space=pltpu.VMEM),
        scratch_shapes=[
            pltpu.VMEM((chunks, n_frame, frames, CH, LANES), BF16),
            pltpu.VMEM((n_frame, rows // 32, 8, LANES), BF16),
            pltpu.VMEM((n_frame, rows // 32, 8, LANES), BF16),
            pltpu.VMEM((2, REACH * n_frame + 1, 8, LANES), BF16),
            pltpu.VMEM((2, REACH * n_frame + 1, 8, LANES), BF16),
            pltpu.VMEM((frames, rows, width), BF16),
            pltpu.VMEM((rows + 2 * REACH, n_frame, 5, 8, LANES), F32),
            pltpu.VMEM((frames * rows, LANES), F32),
            pltpu.VMEM((n_frame * CH * 8, LANES), F32),
            DMA((chunks, n_frame)), DMA((chunks, n_frame)), DMA((chunks,)), DMA,
            DMA((n_frame,)), DMA((n_frame,)), DMA((2,)), DMA((2,)),
        ],
        compiler_params=pltpu.CompilerParams(
            collective_id=0, has_side_effects=True, vmem_limit_bytes=56 * 2**20
        ),
        name="lag_maps",
    )(movie)


def solution(mesh):
    return jax.shard_map(
        body,
        mesh=mesh,
        in_specs=(P("frame", "strip", None),),
        out_specs=P(None, "strip", "frame"),
        check_vma=False,
    )
```

```python
import functools

import jax
import jax.numpy as jnp
from jax import lax
from jax.experimental import pallas as pl
from jax.experimental.pallas import tpu as pltpu
from jax.sharding import PartitionSpec as P

MESH = pl.DeviceIdType.MESH
LANES = 128
CH = 8
REACH = 2
F32 = jnp.float32
BF16 = jnp.bfloat16


def lag_kernel(
    n_frame, n_strip, n_z, frames_total,
    movie, out, block, edges_in, edges_out, rows_in, rows_out, held, spread, picked, work,
    send_sem, recv_sem, own_sem, held_sem, edge_send, edge_recv, row_send, row_recv,
):
    frames, rows, width = movie.shape
    chunks = rows // CH
    n_x = n_frame // n_z
    me = lax.axis_index("frame")
    strip = lax.axis_index("strip")
    z, x = me // n_x, lax.rem(me, n_x)
    inverse = 1.0 / frames_total

    lane = lax.broadcasted_iota(jnp.int32, (8, LANES), 1)
    has_left, has_right = me > 0, me < n_frame - 1

    def peer(k):
        dx, dz = k // n_z, lax.rem(k, n_z)
        return lax.rem(z + dz, n_z) * n_x + lax.rem(x + dx, n_x)

    def chunk_at(step):
        return lax.rem(chunks - step, chunks)

    def columns(g):
        return pl.ds(pl.multiple_of(g * LANES, LANES), LANES)

    def block_copy(c, g, source):
        return pltpu.make_async_remote_copy(
            src_ref=movie.at[:, pl.ds(pl.multiple_of(c * CH, CH), CH), columns(g)],
            dst_ref=block.at[c, source],
            send_sem=send_sem.at[c, g], recv_sem=recv_sem.at[c, source],
            device_id={"frame": g}, device_id_type=MESH,
        )

    def own_copy(c):
        return pltpu.make_async_copy(
            movie.at[:, pl.ds(pl.multiple_of(c * CH, CH), CH), columns(me)],
            block.at[c, me], own_sem.at[c],
        )

    def edge_copy(g, source):
        return pltpu.make_async_remote_copy(
            src_ref=edges_out.at[g], dst_ref=edges_in.at[source],
            send_sem=edge_send.at[g], recv_sem=edge_recv.at[source],
            device_id={"frame": g}, device_id_type=MESH,
        )

    def row_copy(side, to):
        return pltpu.make_async_remote_copy(
            src_ref=rows_out.at[side], dst_ref=rows_in.at[side],
            send_sem=row_send.at[side], recv_sem=row_recv.at[side],
            device_id={"strip": to}, device_id_type=MESH,
        )

    above, below = jnp.maximum(strip - 1, 0), jnp.minimum(strip + 1, n_strip - 1)
    has_above, has_below = strip > 0, strip < n_strip - 1

    whole = pltpu.make_async_copy(movie, held, held_sem)
    whole.start()

    @pl.loop(0, chunks)
    def _(c):
        own_copy(c).start()

    barrier = pltpu.get_barrier_semaphore()

    @pl.loop(1, n_frame)
    def _(k):
        pl.semaphore_signal(barrier, inc=1, device_id={"frame": peer(k)}, device_id_type=MESH)

    @pl.when(has_above)
    def _():
        pl.semaphore_signal(barrier, inc=1, device_id={"strip": above}, device_id_type=MESH)

    @pl.when(has_below)
    def _():
        pl.semaphore_signal(barrier, inc=1, device_id={"strip": below}, device_id_type=MESH)

    neighbours = jnp.where(has_above, 1, 0) + jnp.where(has_below, 1, 0)
    pl.semaphore_wait(barrier, n_frame - 1 + neighbours)

    def send_chunk(step):
        @pl.loop(1, n_frame)
        def _(k):
            block_copy(chunk_at(step), peer(k), me).start()

    send_chunk(0)
    send_chunk(1)

    whole.wait()
    pick_row = lax.broadcasted_iota(jnp.int32, (width, LANES), 0)
    pick_lane = lax.broadcasted_iota(jnp.int32, (width, LANES), 1)
    j = lax.rem(pick_lane, 4)
    target = (pick_lane // 4) * LANES + jnp.where(j < 2, j - 2, LANES - 2 + j)
    pick = jnp.where((pick_row == target) & (pick_lane < 4 * n_frame), 1.0, 0.0).astype(BF16)
    for f in range(frames):
        picked[pl.ds(f * rows, rows), :] = jnp.dot(held[f], pick, preferred_element_type=F32)

    @pl.loop(0, rows, unroll=8)
    def _(r):
        v = picked[pl.ds(r, frames, stride=rows), :]
        work[pl.ds(pl.multiple_of(r * 8, 8), 8), :] = pltpu.roll(v, 4 * lax.rem(r, 32), 1)

    group = lane // 4

    @pl.loop(0, n_frame)
    def _(g):
        for q in range(rows // 32):
            packed = jnp.zeros((8, LANES), F32)
            for r in range(32):
                v = work[pl.ds((q * 32 + r) * 8, 8), :]
                packed = jnp.where(group == lax.rem(r + g, 32), v, packed)
            edges_out[g, q] = pltpu.roll(packed, lax.rem(LANES - 4 * g, LANES), 1).astype(BF16)

    @pl.loop(1, n_frame)
    def _(k):
        edge_copy(peer(k), me).start()

    send_chunk(2)
    send_chunk(3)
    edges_in[me] = edges_out[me]

    @pl.loop(1, n_frame)
    def _(k):
        edge_copy(me, peer(k)).wait_recv()

    beside = ((lane >= LANES - 2) & has_left) | ((lane < 2) & has_right)

    def over_frames(total):
        return jnp.sum(total, axis=0, keepdims=True) * inverse

    def prepare(at, row_of, edge_of, edge_total):
        total = row_of(0)
        for i in range(1, n_frame):
            total = total + row_of(i)
        mean, edge_mean = over_frames(total), over_frames(edge_total)
        for i in range(n_frame):
            value = row_of(i) - mean
            edge = jnp.where(beside, edge_of(i) - edge_mean, 0.0)
            spread[at, i, 2] = value
            spread[at, i, 3] = pltpu.roll(jnp.where(lane < 1, edge, value), LANES - 1, 1)
            spread[at, i, 4] = pltpu.roll(jnp.where(lane < 2, edge, value), LANES - 2, 1)
            spread[at, i, 1] = pltpu.roll(jnp.where(lane >= LANES - 1, edge, value), 1, 1)
            spread[at, i, 0] = pltpu.roll(jnp.where(lane >= LANES - 2, edge, value), 2, 1)

    def work_row(i, r):
        return work[pl.ds(i * CH * 8 + r, 8, stride=CH), :]

    def edge_turn(c, r):
        return lax.rem(2 * LANES - 2 - 4 * (lax.rem(c, 32 // CH) * CH + r), LANES)

    def edge_tile(i, c):
        return edges_in[i, c // (32 // CH)].astype(F32)

    def take_chunk(c):
        @pl.loop(1, n_frame)
        def _(k):
            block_copy(c, me, peer(k)).wait_recv()

        own_copy(c).wait()
        for i in range(n_frame):
            work[pl.ds(i * CH * 8, CH * 8), :] = (
                block[c, i].astype(F32).reshape(CH * 8, LANES)
            )

        @pl.loop(0, CH)
        def _(r):
            turn = edge_turn(c, r)
            edge_total = edge_tile(0, c)
            for i in range(1, n_frame):
                edge_total = edge_total + edge_tile(i, c)
            prepare(
                REACH + c * CH + r,
                lambda i: work_row(i, r),
                lambda i: pltpu.roll(edge_tile(i, c), turn, 1),
                pltpu.roll(edge_total, turn, 1),
            )

    def give_rows(side, c, first):
        packed = jnp.zeros((8, LANES), F32)
        for r in range(REACH):
            for i in range(n_frame):
                rows_out[side, r * n_frame + i] = work_row(i, first + r).astype(BF16)
                place = 4 * (r * n_frame + i)
                turn = lax.rem(edge_turn(c, first + r) + 2 + place, LANES)
                packed = jnp.where(
                    group == place // 4, pltpu.roll(edge_tile(i, c), turn, 1), packed
                )
        rows_out[side, REACH * n_frame] = packed.astype(BF16)

    def take_rows(side, base):
        for r in range(REACH):
            packed = rows_in[side, REACH * n_frame].astype(F32)

            def edge_of(i):
                return pltpu.roll(packed, (2 * LANES - 2 - 4 * (r * n_frame + i)) % LANES, 1)

            edge_total = edge_of(0)
            for i in range(1, n_frame):
                edge_total = edge_total + edge_of(i)
            prepare(
                base + r,
                lambda i: rows_in[side, r * n_frame + i].astype(F32),
                edge_of,
                edge_total,
            )

    def lag_row(r):
        def add(i, sums):
            centre = spread[r + REACH, i, REACH]
            return tuple(
                sums[5 * a + b] + centre * spread[r + a, i, b] for a in range(5) for b in range(5)
            )

        sums = lax.fori_loop(
            0, n_frame, add, tuple(jnp.zeros((8, LANES), F32) for _ in range(25)), unroll=4
        )
        for k in range(25):
            out[k, pl.ds(r, 1), :] = over_frames(sums[k])

    def lag_rows(first, last):
        @pl.loop(first, last)
        def _(r):
            lag_row(r)

    take_chunk(0)
    send_chunk(4)
    give_rows(0, 0, 0)

    @pl.when(has_above)
    def _():
        row_copy(0, above).start()

    take_chunk(chunks - 1)
    send_chunk(5)
    give_rows(1, chunks - 1, CH - REACH)

    @pl.when(has_below)
    def _():
        row_copy(1, below).start()

    lag_rows(REACH, CH - REACH)
    lag_rows(rows - CH + REACH, rows - REACH)

    @pl.loop(2, chunks)
    def _(step):
        c = chunk_at(step)
        take_chunk(c)

        @pl.when(step + 4 < chunks)
        def _():
            send_chunk(step + 4)

        lag_rows(c * CH + REACH, c * CH + CH + REACH)

        @pl.when(step == 2)
        def _():
            zero = jnp.zeros((REACH, n_frame, 5, 8, LANES), F32)

            @pl.when(has_below)
            def _():
                row_copy(0, below).wait_recv()
                take_rows(0, rows + REACH)

            @pl.when(jnp.logical_not(has_below))
            def _():
                spread[rows + REACH : rows + 2 * REACH] = zero

            @pl.when(has_above)
            def _():
                row_copy(1, above).wait_recv()
                take_rows(1, 0)

            @pl.when(jnp.logical_not(has_above))
            def _():
                spread[0:REACH] = zero

            lag_rows(0, REACH)
            lag_rows(rows - REACH, rows)

    lag_rows(CH - REACH, CH + REACH)

    @pl.loop(0, chunks)
    def _(c):
        @pl.loop(1, n_frame)
        def _(k):
            block_copy(c, peer(k), me).wait_send()

    @pl.loop(1, n_frame)
    def _(k):
        edge_copy(peer(k), me).wait_send()

    @pl.when(has_above)
    def _():
        row_copy(0, above).wait_send()

    @pl.when(has_below)
    def _():
        row_copy(1, below).wait_send()


def body(movie):
    frames, rows, width = movie.shape
    n_frame, n_strip = lax.axis_size("frame"), lax.axis_size("strip")
    chunks = rows // CH
    kernel = functools.partial(lag_kernel, n_frame, n_strip, 4, frames * n_frame)
    DMA = pltpu.SemaphoreType.DMA
    return pl.pallas_call(
        kernel,
        out_shape=jax.ShapeDtypeStruct((25, rows, width // n_frame), F32),
        in_specs=[pl.BlockSpec(memory_space=pl.ANY)],
        out_specs=pl.BlockSpec(memory_space=pltpu.VMEM),
        scratch_shapes=[
            pltpu.VMEM((chunks, n_frame, frames, CH, LANES), BF16),
            pltpu.VMEM((n_frame, rows // 32, 8, LANES), BF16),
            pltpu.VMEM((n_frame, rows // 32, 8, LANES), BF16),
            pltpu.VMEM((2, REACH * n_frame + 1, 8, LANES), BF16),
            pltpu.VMEM((2, REACH * n_frame + 1, 8, LANES), BF16),
            pltpu.VMEM((frames, rows, width), BF16),
            pltpu.VMEM((rows + 2 * REACH, n_frame, 5, 8, LANES), F32),
            pltpu.VMEM((frames * rows, LANES), F32),
            pltpu.VMEM((n_frame * CH * 8, LANES), F32),
            DMA((chunks, n_frame)), DMA((chunks, n_frame)), DMA((chunks,)), DMA,
            DMA((n_frame,)), DMA((n_frame,)), DMA((2,)), DMA((2,)),
        ],
        compiler_params=pltpu.CompilerParams(
            collective_id=0, has_side_effects=True, vmem_limit_bytes=56 * 2**20
        ),
        name="lag_maps",
    )(movie)


def solution(mesh):
    return jax.shard_map(
        body,
        mesh=mesh,
        in_specs=(P("frame", "strip", None),),
        out_specs=P(None, "strip", "frame"),
        check_vma=False,
    )
```

```python
import functools

import jax
import jax.numpy as jnp
from jax import lax
from jax.experimental import pallas as pl
from jax.experimental.pallas import tpu as pltpu
from jax.sharding import PartitionSpec as P

MESH = pl.DeviceIdType.MESH
LANES = 128
CH = 8
REACH = 2
F32 = jnp.float32
BF16 = jnp.bfloat16


def lag_kernel(
    n_frame, n_strip, n_z, frames_total,
    movie, out, block, edges_in, edges_out, rows_in, rows_out, held, spread, picked, work,
    send_sem, recv_sem, own_sem, held_sem, edge_send, edge_recv, row_send, row_recv,
):
    frames, rows, width = movie.shape
    chunks = rows // CH
    n_x = n_frame // n_z
    me = lax.axis_index("frame")
    strip = lax.axis_index("strip")
    z, x = me // n_x, lax.rem(me, n_x)
    inverse = 1.0 / frames_total

    lane = lax.broadcasted_iota(jnp.int32, (8, LANES), 1)
    has_left, has_right = me > 0, me < n_frame - 1

    def peer(k):
        dx, dz = k // n_z, lax.rem(k, n_z)
        return lax.rem(z + dz, n_z) * n_x + lax.rem(x + dx, n_x)

    def chunk_at(step):
        return lax.rem(chunks - step, chunks)

    def columns(g):
        return pl.ds(pl.multiple_of(g * LANES, LANES), LANES)

    def block_copy(c, g, source):
        return pltpu.make_async_remote_copy(
            src_ref=movie.at[:, pl.ds(pl.multiple_of(c * CH, CH), CH), columns(g)],
            dst_ref=block.at[c, source],
            send_sem=send_sem, recv_sem=recv_sem.at[c],
            device_id={"frame": g}, device_id_type=MESH,
        )

    def own_copy(c):
        return pltpu.make_async_copy(
            movie.at[:, pl.ds(pl.multiple_of(c * CH, CH), CH), columns(me)],
            block.at[c, me], own_sem,
        )

    def edge_copy(g, source):
        return pltpu.make_async_remote_copy(
            src_ref=edges_out.at[g], dst_ref=edges_in.at[source],
            send_sem=edge_send, recv_sem=edge_recv,
            device_id={"frame": g}, device_id_type=MESH,
        )

    def all_of(ref, sent, received):
        return pltpu.make_async_remote_copy(
            src_ref=ref, dst_ref=ref, send_sem=sent, recv_sem=received,
            device_id={"frame": peer(1)}, device_id_type=MESH,
        )

    def row_copy(side, to):
        return pltpu.make_async_remote_copy(
            src_ref=rows_out.at[side], dst_ref=rows_in.at[side],
            send_sem=row_send.at[side], recv_sem=row_recv.at[side],
            device_id={"strip": to}, device_id_type=MESH,
        )

    above, below = jnp.maximum(strip - 1, 0), jnp.minimum(strip + 1, n_strip - 1)
    has_above, has_below = strip > 0, strip < n_strip - 1

    whole = pltpu.make_async_copy(movie, held, held_sem)
    whole.start()

    @pl.loop(0, chunks)
    def _(c):
        own_copy(c).start()

    barrier = pltpu.get_barrier_semaphore()

    @pl.loop(1, n_frame)
    def _(k):
        pl.semaphore_signal(barrier, inc=1, device_id={"frame": peer(k)}, device_id_type=MESH)

    @pl.when(has_above)
    def _():
        pl.semaphore_signal(barrier, inc=1, device_id={"strip": above}, device_id_type=MESH)

    @pl.when(has_below)
    def _():
        pl.semaphore_signal(barrier, inc=1, device_id={"strip": below}, device_id_type=MESH)

    whole.wait()
    pick_row = lax.broadcasted_iota(jnp.int32, (width, LANES), 0)
    pick_lane = lax.broadcasted_iota(jnp.int32, (width, LANES), 1)
    j = lax.rem(pick_lane, 4)
    target = (pick_lane // 4) * LANES + jnp.where(j < 2, j - 2, LANES - 2 + j)
    pick = jnp.where((pick_row == target) & (pick_lane < 4 * n_frame), 1.0, 0.0).astype(BF16)
    for f in range(frames):
        picked[pl.ds(f * rows, rows), :] = jnp.dot(held[f], pick, preferred_element_type=F32)

    @pl.loop(0, rows, unroll=8)
    def _(r):
        v = picked[pl.ds(r, frames, stride=rows), :]
        work[pl.ds(pl.multiple_of(r * 8, 8), 8), :] = pltpu.roll(v, 4 * lax.rem(r, 32), 1)

    group = lane // 4

    @pl.loop(0, n_frame)
    def _(g):
        for q in range(rows // 32):
            packed = jnp.zeros((8, LANES), F32)
            for r in range(32):
                v = work[pl.ds((q * 32 + r) * 8, 8), :]
                packed = jnp.where(group == lax.rem(r + g, 32), v, packed)
            edges_out[g, q] = pltpu.roll(packed, lax.rem(LANES - 4 * g, LANES), 1).astype(BF16)

    neighbours = jnp.where(has_above, 1, 0) + jnp.where(has_below, 1, 0)
    pl.semaphore_wait(barrier, n_frame - 1 + neighbours)

    def send_chunk(step):
        @pl.loop(1, n_frame)
        def _(k):
            block_copy(chunk_at(step), peer(k), me).start()


    @pl.loop(1, n_frame)
    def _(k):
        edge_copy(peer(k), me).start()

    send_chunk(0)
    send_chunk(1)
    send_chunk(2)
    send_chunk(3)
    edges_in[me] = edges_out[me]

    @pl.loop(0, chunks)
    def _(c):
        own_copy(c).wait()

    beside = ((lane >= LANES - 2) & has_left) | ((lane < 2) & has_right)

    def over_frames(total):
        return jnp.sum(total, axis=0, keepdims=True) * inverse

    def prepare(at, row_of, edge_of, edge_total):
        total = row_of(0)
        for i in range(1, n_frame):
            total = total + row_of(i)
        mean, edge_mean = over_frames(total), over_frames(edge_total)
        for i in range(n_frame):
            value = row_of(i) - mean
            edge = jnp.where(beside, edge_of(i) - edge_mean, 0.0)
            spread[at, i, 2] = value
            spread[at, i, 3] = pltpu.roll(jnp.where(lane < 1, edge, value), LANES - 1, 1)
            spread[at, i, 4] = pltpu.roll(jnp.where(lane < 2, edge, value), LANES - 2, 1)
            spread[at, i, 1] = pltpu.roll(jnp.where(lane >= LANES - 1, edge, value), 1, 1)
            spread[at, i, 0] = pltpu.roll(jnp.where(lane >= LANES - 2, edge, value), 2, 1)

    def work_row(i, r):
        return work[pl.ds(i * CH * 8 + r, 8, stride=CH), :]

    def edge_turn(c, r):
        return lax.rem(2 * LANES - 2 - 4 * (lax.rem(c, 32 // CH) * CH + r), LANES)

    def edge_tile(i, c):
        return edges_in[i, c // (32 // CH)].astype(F32)

    def take_chunk(step):
        c = chunk_at(step)

        all_of(block.at[c, pl.ds(0, n_frame - 1)], send_sem, recv_sem.at[c]).wait_recv()

        @pl.when(step + 4 < chunks)
        def _():
            send_chunk(step + 4)

        for i in range(n_frame):
            work[pl.ds(i * CH * 8, CH * 8), :] = (
                block[c, i].astype(F32).reshape(CH * 8, LANES)
            )

        @pl.when(step == 0)
        def _():
            all_of(edges_in.at[pl.ds(0, n_frame - 1)], edge_send, edge_recv).wait_recv()

        @pl.loop(0, CH)
        def _(r):
            turn = edge_turn(c, r)
            edge_total = edge_tile(0, c)
            for i in range(1, n_frame):
                edge_total = edge_total + edge_tile(i, c)
            prepare(
                REACH + c * CH + r,
                lambda i: work_row(i, r),
                lambda i: pltpu.roll(edge_tile(i, c), turn, 1),
                pltpu.roll(edge_total, turn, 1),
            )

    def give_rows(side, c, first):
        packed = jnp.zeros((8, LANES), F32)
        for r in range(REACH):
            for i in range(n_frame):
                rows_out[side, r * n_frame + i] = work_row(i, first + r).astype(BF16)
                place = 4 * (r * n_frame + i)
                turn = lax.rem(edge_turn(c, first + r) + 2 + place, LANES)
                packed = jnp.where(
                    group == place // 4, pltpu.roll(edge_tile(i, c), turn, 1), packed
                )
        rows_out[side, REACH * n_frame] = packed.astype(BF16)

    def take_rows(side, base):
        for r in range(REACH):
            packed = rows_in[side, REACH * n_frame].astype(F32)

            def edge_of(i):
                return pltpu.roll(packed, (2 * LANES - 2 - 4 * (r * n_frame + i)) % LANES, 1)

            edge_total = edge_of(0)
            for i in range(1, n_frame):
                edge_total = edge_total + edge_of(i)
            prepare(
                base + r,
                lambda i: rows_in[side, r * n_frame + i].astype(F32),
                edge_of,
                edge_total,
            )

    def lag_row(r):
        def add(i, sums):
            centre = spread[r + REACH, i, REACH]
            return tuple(
                sums[5 * a + b] + centre * spread[r + a, i, b] for a in range(5) for b in range(5)
            )

        sums = lax.fori_loop(
            0, n_frame, add, tuple(jnp.zeros((8, LANES), F32) for _ in range(25)), unroll=4
        )
        for k in range(25):
            out[k, pl.ds(r, 1), :] = over_frames(sums[k])

    def lag_rows(first, last):
        @pl.loop(first, last)
        def _(r):
            lag_row(r)

    take_chunk(0)
    give_rows(0, 0, 0)

    @pl.when(has_above)
    def _():
        row_copy(0, above).start()

    take_chunk(1)
    give_rows(1, chunks - 1, CH - REACH)

    @pl.when(has_below)
    def _():
        row_copy(1, below).start()

    lag_rows(REACH, CH - REACH)
    lag_rows(rows - CH + REACH, rows - REACH)

    @pl.loop(2, chunks)
    def _(step):
        c = chunk_at(step)
        take_chunk(step)

        lag_rows(c * CH + REACH, c * CH + CH + REACH)

        @pl.when(step == 2)
        def _():
            zero = jnp.zeros((REACH, n_frame, 5, 8, LANES), F32)

            @pl.when(has_below)
            def _():
                row_copy(0, below).wait_recv()
                take_rows(0, rows + REACH)

            @pl.when(jnp.logical_not(has_below))
            def _():
                spread[rows + REACH : rows + 2 * REACH] = zero

            @pl.when(has_above)
            def _():
                row_copy(1, above).wait_recv()
                take_rows(1, 0)

            @pl.when(jnp.logical_not(has_above))
            def _():
                spread[0:REACH] = zero

            lag_rows(0, REACH)
            lag_rows(rows - REACH, rows)

    lag_rows(CH - REACH, CH + REACH)

    all_of(block.at[:, pl.ds(0, n_frame - 1)], send_sem, recv_sem.at[0]).wait_send()
    all_of(edges_in.at[pl.ds(0, n_frame - 1)], edge_send, edge_recv).wait_send()

    @pl.when(has_above)
    def _():
        row_copy(0, above).wait_send()

    @pl.when(has_below)
    def _():
        row_copy(1, below).wait_send()


def body(movie):
    frames, rows, width = movie.shape
    n_frame, n_strip = lax.axis_size("frame"), lax.axis_size("strip")
    chunks = rows // CH
    kernel = functools.partial(lag_kernel, n_frame, n_strip, 4, frames * n_frame)
    DMA = pltpu.SemaphoreType.DMA
    return pl.pallas_call(
        kernel,
        out_shape=jax.ShapeDtypeStruct((25, rows, width // n_frame), F32),
        in_specs=[pl.BlockSpec(memory_space=pl.ANY)],
        out_specs=pl.BlockSpec(memory_space=pltpu.VMEM),
        scratch_shapes=[
            pltpu.VMEM((chunks, n_frame, frames, CH, LANES), BF16),
            pltpu.VMEM((n_frame, rows // 32, 8, LANES), BF16),
            pltpu.VMEM((n_frame, rows // 32, 8, LANES), BF16),
            pltpu.VMEM((2, REACH * n_frame + 1, 8, LANES), BF16),
            pltpu.VMEM((2, REACH * n_frame + 1, 8, LANES), BF16),
            pltpu.VMEM((frames, rows, width), BF16),
            pltpu.VMEM((rows + 2 * REACH, n_frame, 5, 8, LANES), F32),
            pltpu.VMEM((frames * rows, LANES), F32),
            pltpu.VMEM((n_frame * CH * 8, LANES), F32),
            DMA, DMA((chunks,)), DMA, DMA,
            DMA, DMA, DMA((2,)), DMA((2,)),
        ],
        compiler_params=pltpu.CompilerParams(
            collective_id=0, has_side_effects=True, vmem_limit_bytes=56 * 2**20
        ),
        name="lag_maps",
    )(movie)


def solution(mesh):
    return jax.shard_map(
        body,
        mesh=mesh,
        in_specs=(P("frame", "strip", None),),
        out_specs=P(None, "strip", "frame"),
        check_vma=False,
    )
```

```python
import functools

import jax
import jax.numpy as jnp
from jax import lax
from jax.experimental import pallas as pl
from jax.experimental.pallas import tpu as pltpu
from jax.sharding import PartitionSpec as P

MESH = pl.DeviceIdType.MESH
LANES = 128
CH = 8
REACH = 2
AHEAD = 4
WRAP = 0
F32 = jnp.float32
BF16 = jnp.bfloat16


def lag_kernel(
    n_frame, n_strip, n_x, frames_total,
    movie, out,
    block, edges_in, edges_out, rows_in, rows_out, held, spread, picked, work,
    reduced, sent, got, means, far_means, totals,
    send_sem, recv_sem, own_sem, held_sem, edge_send, edge_recv, row_send, row_recv,
    part_send, part_recv,
):
    frames, rows, width = movie.shape
    chunks = rows // CH
    n_half = n_frame // 2
    me = lax.axis_index("frame")
    strip = lax.axis_index("strip")
    first = (me // n_half) * n_half
    mine = me - first
    partner = lax.rem(me + n_half, n_frame)
    inverse = 1.0 / frames_total

    lane = lax.broadcasted_iota(jnp.int32, (8, LANES), 1)
    sub = lax.broadcasted_iota(jnp.int32, (8, LANES), 0)
    group = lane // 4
    zero = jnp.zeros((8, LANES), F32)

    def peer(k):
        dx, dz = k // 2, lax.rem(k, 2)
        return lax.rem(mine // n_x + dz, 2) * n_x + lax.rem(lax.rem(mine, n_x) + dx, n_x)

    def chunk_at(step):
        return lax.rem(chunks - step, chunks)

    def owner(slot, index):
        return lax.rem(first + index + (1 - slot) * n_half, n_frame)

    def tile(c, g):
        return movie.at[
            :, pl.ds(pl.multiple_of(c * CH, CH), CH),
            pl.ds(pl.multiple_of(g * LANES, LANES), LANES),
        ]

    def own_copy(c, slot):
        return pltpu.make_async_copy(tile(c, owner(slot, mine)), block.at[c, slot, mine], own_sem)

    def to_peer(src, dst, send, recv, index):
        return pltpu.make_async_remote_copy(
            src_ref=src, dst_ref=dst, send_sem=send, recv_sem=recv,
            device_id={"frame": first + index}, device_id_type=MESH,
        )

    def all_of(ref, send, recv):
        return to_peer(ref, ref, send, recv, peer(1))

    def to_partner(at, count):
        return pltpu.make_async_remote_copy(
            src_ref=sent.at[pl.ds(at, count)], dst_ref=got.at[pl.ds(at, count)],
            send_sem=part_send, recv_sem=part_recv.at[at],
            device_id={"frame": partner}, device_id_type=MESH,
        )

    def row_copy(side, to):
        return pltpu.make_async_remote_copy(
            src_ref=rows_out.at[side], dst_ref=rows_in.at[side],
            send_sem=row_send.at[side], recv_sem=row_recv.at[side],
            device_id={"strip": to}, device_id_type=MESH,
        )

    above, below = jnp.maximum(strip - 1, 0), jnp.minimum(strip + 1, n_strip - 1)
    has_above, has_below = strip > 0, strip < n_strip - 1

    whole = pltpu.make_async_copy(movie, held, held_sem)
    whole.start()

    @pl.loop(0, chunks)
    def _(c):
        own_copy(c, 0).start()
        own_copy(c, 1).start()

    barrier = pltpu.get_barrier_semaphore()

    @pl.loop(1, n_half)
    def _(k):
        pl.semaphore_signal(
            barrier, inc=1, device_id={"frame": first + peer(k)}, device_id_type=MESH
        )

    pl.semaphore_signal(barrier, inc=1, device_id={"frame": partner}, device_id_type=MESH)

    @pl.when(has_above)
    def _():
        pl.semaphore_signal(barrier, inc=1, device_id={"strip": above}, device_id_type=MESH)

    @pl.when(has_below)
    def _():
        pl.semaphore_signal(barrier, inc=1, device_id={"strip": below}, device_id_type=MESH)

    totals[...] = jnp.zeros(totals.shape, F32)
    means[...] = jnp.zeros(means.shape, F32)

    whole.wait()
    pick_row = lax.broadcasted_iota(jnp.int32, (width, LANES), 0)
    pick_lane = lax.broadcasted_iota(jnp.int32, (width, LANES), 1)
    j = lax.rem(pick_lane, 4)
    target = (pick_lane // 4) * LANES + jnp.where(j < 2, j - 2, LANES - 2 + j)
    pick = jnp.where((pick_row == target) & (pick_lane < 4 * n_frame), 1.0, 0.0).astype(BF16)
    for f in range(frames):
        picked[pl.ds(f * rows, rows), :] = jnp.dot(held[f], pick, preferred_element_type=F32)

    @pl.loop(0, rows, unroll=8)
    def _(r):
        v = picked[pl.ds(r, frames, stride=rows), :]
        work[pl.ds(pl.multiple_of(r * 8, 8), 8), :] = pltpu.roll(v, 4 * lax.rem(r, 32), 1)

    @pl.loop(0, n_frame)
    def _(g):
        for q in range(rows // 32):
            packed = zero
            for r in range(32):
                v = work[pl.ds((q * 32 + r) * 8, 8), :]
                packed = jnp.where(group == lax.rem(r + g, 32), v, packed)
            edges_out[g, q] = pltpu.roll(packed, lax.rem(LANES - 4 * g, LANES), 1).astype(BF16)

    neighbours = jnp.where(has_above, 1, 0) + jnp.where(has_below, 1, 0)
    pl.semaphore_wait(barrier, n_half + neighbours)

    def send_chunk(step):
        c = chunk_at(step)

        @pl.loop(1, n_half)
        def _(k):
            p = peer(k)
            for slot in range(2):
                to_peer(
                    tile(c, owner(slot, p)), block.at[c, slot, mine],
                    send_sem, recv_sem.at[c], p,
                ).start()

    @pl.loop(1, n_half)
    def _(k):
        p = peer(k)
        for slot in range(2):
            to_peer(
                edges_out.at[owner(slot, p)], edges_in.at[slot, mine], edge_send, edge_recv, p
            ).start()

    for step in range(AHEAD):
        send_chunk(step)
    for slot in range(2):
        edges_in[slot, mine] = edges_out[owner(slot, mine)]

    @pl.loop(0, chunks)
    def _(c):
        own_copy(c, 0).wait()
        own_copy(c, 1).wait()

    beside = []
    for slot in range(2):
        g = owner(slot, mine)
        beside.append(((lane >= LANES - 2) & (g > 0)) | ((lane < 2) & (g < n_frame - 1)))

    def shifted(value, edge, b):
        if b == 0:
            return value
        near = lane < b if b > 0 else lane >= LANES + b
        return pltpu.roll(jnp.where(near, edge, value), (LANES - b) % LANES, 1)

    def over_frames(total):
        return jnp.sum(total, axis=0, keepdims=True) * (1.0 / (n_half * frames))

    def prepare(slot, r, row_of, edge_of, edge_total):
        total = row_of(0)
        for i in range(1, n_half):
            total = total + row_of(i)
        mean, edge_mean = over_frames(total), over_frames(edge_total)
        means[slot, 0, pl.ds(r + 8, 1), :] = mean
        means[slot, 1, pl.ds(r + 8, 1), :] = jnp.where(beside[slot][:1], edge_mean, 0.0)
        for i in range(n_half):
            value = row_of(i) - mean
            edge = jnp.where(beside[slot], edge_of(i) - edge_mean, 0.0)
            for b in range(-REACH, REACH + 1):
                spread[slot, r + REACH, i, b + REACH] = shifted(value, edge, b)

    def work_row(slot, i, r):
        return work[pl.ds((slot * n_half + i) * CH * 8 + r, 8, stride=CH), :]

    def edge_turn(c, r):
        return lax.rem(2 * LANES - 2 - 4 * (lax.rem(c, 32 // CH) * CH + r), LANES)

    def edge_tile(slot, i, c):
        return edges_in[slot, i, c // (32 // CH)].astype(F32)

    def take_chunk(step):
        c = chunk_at(step)
        all_of(block.at[c, :, pl.ds(0, n_half - 1)], send_sem, recv_sem.at[c]).wait_recv()

        @pl.when(step + AHEAD < chunks)
        def _():
            send_chunk(step + AHEAD)

        for slot in range(2):
            for i in range(n_half):
                work[pl.ds((slot * n_half + i) * CH * 8, CH * 8), :] = (
                    block[c, slot, i].astype(F32).reshape(CH * 8, LANES)
                )

        @pl.when(step == 0)
        def _():
            all_of(edges_in.at[:, pl.ds(0, n_half - 1)], edge_send, edge_recv).wait_recv()

        edge_totals = []
        for slot in range(2):
            edge_total = edge_tile(slot, 0, c)
            for i in range(1, n_half):
                edge_total = edge_total + edge_tile(slot, i, c)
            edge_totals.append(edge_total)

        @pl.loop(0, CH, unroll=2)
        def _(r):
            turn = edge_turn(c, r)
            for slot in range(2):
                prepare(
                    slot, c * CH + r,
                    lambda i: work_row(slot, i, r),
                    lambda i: pltpu.roll(edge_tile(slot, i, c), turn, 1),
                    pltpu.roll(edge_totals[slot], turn, 1),
                )

    def place(slot, r, i):
        return (slot * REACH + r) * n_half + i

    def give_rows(side, c, start):
        packed = zero
        for slot in range(2):
            for r in range(REACH):
                for i in range(n_half):
                    at = place(slot, r, i)
                    rows_out[side, at] = work_row(slot, i, start + r).astype(BF16)
                    turn = lax.rem(edge_turn(c, start + r) + 2 + 4 * at, LANES)
                    packed = jnp.where(
                        group == at, pltpu.roll(edge_tile(slot, i, c), turn, 1), packed
                    )
        rows_out[side, 2 * REACH * n_half] = packed.astype(BF16)

    def take_rows(side, base):
        packed = rows_in[side, 2 * REACH * n_half].astype(F32)
        for slot in range(2):
            for r in range(REACH):

                def edge_of(i):
                    turn = (2 * LANES - 2 - 4 * place(slot, r, i)) % LANES
                    return pltpu.roll(packed, turn, 1)

                edge_total = edge_of(0)
                for i in range(1, n_half):
                    edge_total = edge_total + edge_of(i)
                prepare(
                    slot, base + r,
                    lambda i: rows_in[side, place(slot, r, i)].astype(F32),
                    edge_of, edge_total,
                )

    def lag_group(slot, start):
        @pl.loop(0, CH)
        def _(n):
            r = lax.rem(start + n, rows)
            sums = [None] * 25
            for i in range(n_half):
                centre = spread[slot, r + REACH, i, REACH]
                for k in range(25):
                    term = centre * spread[slot, r + k // 5, i, k % 5]
                    sums[k] = term if i == 0 else sums[k] + term
            for k in range(25):
                reduced[k, pl.ds(pl.multiple_of(n * 8, 8), 8), :] = sums[k]

    def lag_plane(k):
        total = reduced[k, pl.ds(0, CH, stride=8), :]
        for n in range(1, 8):
            total = total + reduced[k, pl.ds(n, CH, stride=8), :]
        return total * inverse

    def pack_planes(at):
        for p in range(13):
            sent[at, p] = lag_plane(12 + p)
        side = zero
        for k in range(12):
            plane = lag_plane(k)
            if k % 5 != REACH:
                side = jnp.where(group == k, pltpu.roll(plane, 4 * k + 2, 1), side)
            if at is WRAP:
                sent[at + 1, k] = plane
        sent[at, 13] = side

    def mean_rows(c):
        return pl.ds(pl.multiple_of(8 + c * CH, CH), CH)

    def send_group(at, c):
        lag_group(0, c * CH + REACH)
        pack_planes(at)
        for kind in range(2):
            sent[at, 14 + kind] = means[0, kind, mean_rows(c), :]
        to_partner(at, 1).start()

    def send_wrap():
        lag_group(0, rows - CH + REACH)
        pack_planes(WRAP)
        for kind in range(2):
            sent[WRAP, 14 + kind] = means[0, kind, mean_rows(0), :]
            sent[WRAP + 1, 12 + kind] = means[0, kind, mean_rows(chunks - 1), :]
            sent[WRAP + 1, 14 + kind] = (
                means[0, kind, pl.ds(0, 8), :] + means[0, kind, pl.ds(8 + rows, 8), :]
            )
        to_partner(WRAP, 2).start()

    def add(k, at, value, keep=None):
        if keep is not None:
            value = jnp.where(keep, value, 0.0)
        totals[k, pl.ds(at, 8), :] += value

    wrapped = ((rows - CH + REACH, sub < CH - REACH), (REACH - CH, sub >= CH - REACH))

    def own_group(c):
        lag_group(1, c * CH + REACH)
        for k in range(25):
            add(k, 8 + c * CH + REACH, lag_plane(k))

    def own_wrap():
        lag_group(1, rows - CH + REACH)
        for k in range(25):
            plane = lag_plane(k)
            for start, keep in wrapped:
                add(k, 8 + start, plane, keep)

    def add_far(at, base, keep=None):
        gap = {}
        for a in range(-REACH, REACH + 1):
            value, edge = (
                means[1, kind, pl.ds(base + a, 8), :] - far_means[kind, pl.ds(base + a, 8), :]
                for kind in range(2)
            )
            for b in range(-REACH, REACH + 1):
                gap[a, b] = shifted(value, edge, b)
        centre = gap[0, 0] * 0.25
        side = got[at, 13]
        for k in range(25):
            a, b = k // 5 - REACH, k % 5 - REACH
            value = centre * gap[a, b]
            if k >= 12:
                plane = got[at, k - 12]
                value = value + plane
                if k > 12:
                    moved = pltpu.roll(plane, b % LANES, 1)
                    inside = (lane >= b) & (lane < LANES + b)
                    add(24 - k, base + a, jnp.where(inside, moved, 0.0), keep)
            else:
                if b != 0:
                    column = pltpu.roll(side, (2 * LANES - 4 * k - 2) % LANES, 1)
                    outside = (lane < -b) | (lane >= LANES - b)
                    if keep is not None:
                        outside = outside & (sub != 6 if a == -1 else sub < 6) if a < 0 else outside
                    value = value + jnp.where(outside, column, 0.0)
                if keep is not None and a < 0:
                    direct = sub == 6 if a == -1 else sub >= 6
                    value = value + jnp.where(direct, got[at + 1, k], 0.0)
            add(k, base, value, keep)

    def take_group(at, c):
        to_partner(at, 1).wait_recv()
        for kind in range(2):
            far_means[kind, mean_rows(c), :] = got[at, 14 + kind]
        add_far(at, 8 + c * CH + REACH)

    def take_wrap():
        to_partner(WRAP, 2).wait_recv()
        for kind in range(2):
            far_means[kind, mean_rows(0), :] = got[WRAP, 14 + kind]
            far_means[kind, mean_rows(chunks - 1), :] = got[WRAP + 1, 12 + kind]
            ends = got[WRAP + 1, 14 + kind]
            far_means[kind, pl.ds(0, 8), :] = jnp.where(sub >= 8 - REACH, ends, 0.0)
            far_means[kind, pl.ds(8 + rows, 8), :] = jnp.where(sub < REACH, ends, 0.0)
        for start, keep in wrapped:
            add_far(WRAP, 8 + start, keep)

    take_chunk(0)
    give_rows(0, 0, 0)

    @pl.when(has_above)
    def _():
        row_copy(0, above).start()

    take_chunk(1)
    give_rows(1, chunks - 1, CH - REACH)

    @pl.when(has_below)
    def _():
        row_copy(1, below).start()

    @pl.loop(2, chunks - 1)
    def _(step):
        c = chunk_at(step)
        take_chunk(step)

        @pl.when(step == 3)
        def _():
            empty = jnp.zeros((2, REACH, n_half, 5, 8, LANES), F32)

            @pl.when(has_below)
            def _():
                row_copy(0, below).wait_recv()
                take_rows(0, rows)

            @pl.when(jnp.logical_not(has_below))
            def _():
                spread[:, rows + REACH : rows + 2 * REACH] = empty

            @pl.when(has_above)
            def _():
                row_copy(1, above).wait_recv()
                take_rows(1, -REACH)

            @pl.when(jnp.logical_not(has_above))
            def _():
                spread[:, 0:REACH] = empty

            send_wrap()

        send_group(step, c)
        own_group(c)

        @pl.when(step == 3)
        def _():
            own_wrap()

        @pl.when(step == 4)
        def _():
            take_wrap()

        @pl.when(step >= 4)
        def _():
            take_group(step - 2, chunk_at(step - 2))

    last = chunks - 1
    take_chunk(last)
    send_group(last, 1)
    send_group(last + 1, 0)
    own_group(1)
    take_group(last - 2, 3)
    take_group(last - 1, 2)
    own_group(0)
    take_group(last, 1)
    take_group(last + 1, 0)
    out[...] = totals[:, 8 : 8 + rows, :]

    all_of(block.at[:, :, pl.ds(0, n_half - 1)], send_sem, recv_sem.at[0]).wait_send()
    all_of(edges_in.at[:, pl.ds(0, n_half - 1)], edge_send, edge_recv).wait_send()
    to_partner(0, chunks + 1).wait_send()

    @pl.when(has_above)
    def _():
        row_copy(0, above).wait_send()

    @pl.when(has_below)
    def _():
        row_copy(1, below).wait_send()


def body(movie):
    frames, rows, width = movie.shape
    n_frame, n_strip = lax.axis_size("frame"), lax.axis_size("strip")
    chunks, n_half = rows // CH, n_frame // 2
    kernel = functools.partial(lag_kernel, n_frame, n_strip, 4, frames * n_frame)
    DMA = pltpu.SemaphoreType.DMA
    padded = rows + 16
    return pl.pallas_call(
        kernel,
        out_shape=jax.ShapeDtypeStruct((25, rows, width // n_frame), F32),
        in_specs=[pl.BlockSpec(memory_space=pl.ANY)],
        out_specs=pl.BlockSpec(memory_space=pltpu.VMEM),
        scratch_shapes=[
            pltpu.VMEM((chunks, 2, n_half, frames, CH, LANES), BF16),
            pltpu.VMEM((2, n_half, rows // 32, 8, LANES), BF16),
            pltpu.VMEM((n_frame, rows // 32, 8, LANES), BF16),
            pltpu.VMEM((2, 2 * REACH * n_half + 1, 8, LANES), BF16),
            pltpu.VMEM((2, 2 * REACH * n_half + 1, 8, LANES), BF16),
            pltpu.VMEM((frames, rows, width), BF16),
            pltpu.VMEM((2, rows + 2 * REACH, n_half, 5, 8, LANES), F32),
            pltpu.VMEM((frames * rows, LANES), F32),
            pltpu.VMEM((n_frame * CH * 8, LANES), F32),
            pltpu.VMEM((25, CH * 8, LANES), F32),
            pltpu.VMEM((chunks + 1, 16, 8, LANES), F32),
            pltpu.VMEM((chunks + 1, 16, 8, LANES), F32),
            pltpu.VMEM((2, 2, padded, LANES), F32),
            pltpu.VMEM((2, padded, LANES), F32),
            pltpu.VMEM((25, padded, LANES), F32),
            DMA, DMA((chunks,)), DMA, DMA, DMA, DMA, DMA((2,)), DMA((2,)),
            DMA, DMA((chunks + 1,)),
        ],
        compiler_params=pltpu.CompilerParams(
            collective_id=0, has_side_effects=True, vmem_limit_bytes=56 * 2**20
        ),
        name="lag_maps",
    )(movie)


def solution(mesh):
    return jax.shard_map(
        body,
        mesh=mesh,
        in_specs=(P("frame", "strip", None),),
        out_specs=P(None, "strip", "frame"),
        check_vma=False,
    )
```

```python
import functools

import jax
import jax.numpy as jnp
from jax import lax
from jax.experimental import pallas as pl
from jax.experimental.pallas import tpu as pltpu
from jax.sharding import PartitionSpec as P

MESH = pl.DeviceIdType.MESH
LANES = 128
CH = 8
REACH = 2
AHEAD = 2
WRAP = 0
F32 = jnp.float32
BF16 = jnp.bfloat16


def lag_kernel(
    n_frame, n_strip, n_x, frames_total,
    movie, out,
    block, edges_in, edges_out, rows_in, rows_out, held, spread, picked, work,
    reduced, sent, got, means, far_means, totals,
    send_sem, recv_sem, own_sem, held_sem, edge_send, edge_recv, row_send, row_recv,
    part_send, part_recv,
):
    frames, rows, width = movie.shape
    chunks = rows // CH
    n_half = n_frame // 2
    me = lax.axis_index("frame")
    strip = lax.axis_index("strip")
    first = (me // n_half) * n_half
    mine = me - first
    partner = lax.rem(me + n_half, n_frame)
    inverse = 1.0 / frames_total

    lane = lax.broadcasted_iota(jnp.int32, (8, LANES), 1)
    sub = lax.broadcasted_iota(jnp.int32, (8, LANES), 0)
    group = lane // 4
    zero = jnp.zeros((8, LANES), F32)

    def peer(k):
        dx, dz = k // 2, lax.rem(k, 2)
        return lax.rem(mine // n_x + dz, 2) * n_x + lax.rem(lax.rem(mine, n_x) + dx, n_x)

    def chunk_at(step):
        return lax.rem(chunks - step, chunks)

    def owner(slot, index):
        return lax.rem(first + index + (1 - slot) * n_half, n_frame)

    def tile(c, g):
        return movie.at[
            :, pl.ds(pl.multiple_of(c * CH, CH), CH),
            pl.ds(pl.multiple_of(g * LANES, LANES), LANES),
        ]

    def own_copy(c, slot):
        return pltpu.make_async_copy(tile(c, owner(slot, mine)), block.at[c, slot, mine], own_sem)

    def to_peer(src, dst, send, recv, index):
        return pltpu.make_async_remote_copy(
            src_ref=src, dst_ref=dst, send_sem=send, recv_sem=recv,
            device_id={"frame": first + index}, device_id_type=MESH,
        )

    def all_of(ref, send, recv):
        return to_peer(ref, ref, send, recv, peer(1))

    def to_partner(at, count):
        return pltpu.make_async_remote_copy(
            src_ref=sent.at[pl.ds(at, count)], dst_ref=got.at[pl.ds(at, count)],
            send_sem=part_send, recv_sem=part_recv.at[at],
            device_id={"frame": partner}, device_id_type=MESH,
        )

    def row_copy(side, to):
        return pltpu.make_async_remote_copy(
            src_ref=rows_out.at[side], dst_ref=rows_in.at[side],
            send_sem=row_send.at[side], recv_sem=row_recv.at[side],
            device_id={"strip": to}, device_id_type=MESH,
        )

    above, below = jnp.maximum(strip - 1, 0), jnp.minimum(strip + 1, n_strip - 1)
    has_above, has_below = strip > 0, strip < n_strip - 1

    whole = pltpu.make_async_copy(movie, held, held_sem)
    whole.start()

    @pl.loop(0, chunks)
    def _(c):
        own_copy(c, 0).start()
        own_copy(c, 1).start()

    barrier = pltpu.get_barrier_semaphore()

    @pl.loop(1, n_half)
    def _(k):
        pl.semaphore_signal(
            barrier, inc=1, device_id={"frame": first + peer(k)}, device_id_type=MESH
        )

    pl.semaphore_signal(barrier, inc=1, device_id={"frame": partner}, device_id_type=MESH)

    @pl.when(has_above)
    def _():
        pl.semaphore_signal(barrier, inc=1, device_id={"strip": above}, device_id_type=MESH)

    @pl.when(has_below)
    def _():
        pl.semaphore_signal(barrier, inc=1, device_id={"strip": below}, device_id_type=MESH)

    totals[...] = jnp.zeros(totals.shape, F32)
    means[...] = jnp.zeros(means.shape, F32)

    whole.wait()
    pick_row = lax.broadcasted_iota(jnp.int32, (width, LANES), 0)
    pick_lane = lax.broadcasted_iota(jnp.int32, (width, LANES), 1)
    j = lax.rem(pick_lane, 4)
    target = (pick_lane // 4) * LANES + jnp.where(j < 2, j - 2, LANES - 2 + j)
    pick = jnp.where((pick_row == target) & (pick_lane < 4 * n_frame), 1.0, 0.0).astype(BF16)
    for f in range(frames):
        picked[pl.ds(f * rows, rows), :] = jnp.dot(held[f], pick, preferred_element_type=F32)

    @pl.loop(0, rows, unroll=8)
    def _(r):
        v = picked[pl.ds(r, frames, stride=rows), :]
        work[pl.ds(pl.multiple_of(r * 8, 8), 8), :] = pltpu.roll(v, 4 * lax.rem(r, 32), 1)

    @pl.loop(0, n_frame)
    def _(g):
        for q in range(rows // 32):
            packed = zero
            for r in range(32):
                v = work[pl.ds((q * 32 + r) * 8, 8), :]
                packed = jnp.where(group == lax.rem(r + g, 32), v, packed)
            edges_out[g, q] = pltpu.roll(packed, lax.rem(LANES - 4 * g, LANES), 1).astype(BF16)

    neighbours = jnp.where(has_above, 1, 0) + jnp.where(has_below, 1, 0)
    pl.semaphore_wait(barrier, n_half + neighbours)

    def send_chunk(step):
        c = chunk_at(step)

        @pl.loop(1, n_half)
        def _(k):
            p = peer(k)
            for slot in range(2):
                to_peer(
                    tile(c, owner(slot, p)), block.at[c, slot, mine],
                    send_sem, recv_sem.at[c], p,
                ).start()

    @pl.loop(1, n_half)
    def _(k):
        p = peer(k)
        for slot in range(2):
            to_peer(
                edges_out.at[owner(slot, p)], edges_in.at[slot, mine], edge_send, edge_recv, p
            ).start()

    for step in range(AHEAD):
        send_chunk(step)
    for slot in range(2):
        edges_in[slot, mine] = edges_out[owner(slot, mine)]

    @pl.loop(0, chunks)
    def _(c):
        own_copy(c, 0).wait()
        own_copy(c, 1).wait()

    beside = []
    for slot in range(2):
        g = owner(slot, mine)
        beside.append(((lane >= LANES - 2) & (g > 0)) | ((lane < 2) & (g < n_frame - 1)))

    def shifted(value, edge, b):
        if b == 0:
            return value
        near = lane < b if b > 0 else lane >= LANES + b
        return pltpu.roll(jnp.where(near, edge, value), (LANES - b) % LANES, 1)

    def over_frames(total):
        return jnp.sum(total, axis=0, keepdims=True) * (1.0 / (n_half * frames))

    def prepare(slot, r, row_of, edge_of, edge_total):
        total = row_of(0)
        for i in range(1, n_half):
            total = total + row_of(i)
        mean, edge_mean = over_frames(total), over_frames(edge_total)
        means[slot, 0, pl.ds(r + 8, 1), :] = mean
        means[slot, 1, pl.ds(r + 8, 1), :] = jnp.where(beside[slot][:1], edge_mean, 0.0)
        for i in range(n_half):
            value = row_of(i) - mean
            edge = jnp.where(beside[slot], edge_of(i) - edge_mean, 0.0)
            for b in range(-REACH, REACH + 1):
                spread[slot, r + REACH, i, b + REACH] = shifted(value, edge, b)

    def work_row(slot, i, r):
        return work[pl.ds((slot * n_half + i) * CH * 8 + r, 8, stride=CH), :]

    def edge_turn(c, r):
        return lax.rem(2 * LANES - 2 - 4 * (lax.rem(c, 32 // CH) * CH + r), LANES)

    def edge_tile(slot, i, c):
        return edges_in[slot, i, c // (32 // CH)].astype(F32)

    def take_chunk(step):
        c = chunk_at(step)
        all_of(block.at[c, :, pl.ds(0, n_half - 1)], send_sem, recv_sem.at[c]).wait_recv()

        @pl.when(step + AHEAD < chunks)
        def _():
            send_chunk(step + AHEAD)

        for slot in range(2):
            for i in range(n_half):
                work[pl.ds((slot * n_half + i) * CH * 8, CH * 8), :] = (
                    block[c, slot, i].astype(F32).reshape(CH * 8, LANES)
                )

        @pl.when(step == 0)
        def _():
            all_of(edges_in.at[:, pl.ds(0, n_half - 1)], edge_send, edge_recv).wait_recv()

        edge_totals = []
        for slot in range(2):
            edge_total = edge_tile(slot, 0, c)
            for i in range(1, n_half):
                edge_total = edge_total + edge_tile(slot, i, c)
            edge_totals.append(edge_total)

        @pl.loop(0, CH, unroll=2)
        def _(r):
            turn = edge_turn(c, r)
            for slot in range(2):
                prepare(
                    slot, c * CH + r,
                    lambda i: work_row(slot, i, r),
                    lambda i: pltpu.roll(edge_tile(slot, i, c), turn, 1),
                    pltpu.roll(edge_totals[slot], turn, 1),
                )

    def place(slot, r, i):
        return (slot * REACH + r) * n_half + i

    def give_rows(side, c, start):
        packed = zero
        for slot in range(2):
            for r in range(REACH):
                for i in range(n_half):
                    at = place(slot, r, i)
                    rows_out[side, at] = work_row(slot, i, start + r).astype(BF16)
                    turn = lax.rem(edge_turn(c, start + r) + 2 + 4 * at, LANES)
                    packed = jnp.where(
                        group == at, pltpu.roll(edge_tile(slot, i, c), turn, 1), packed
                    )
        rows_out[side, 2 * REACH * n_half] = packed.astype(BF16)

    def take_rows(side, base):
        packed = rows_in[side, 2 * REACH * n_half].astype(F32)
        for slot in range(2):
            for r in range(REACH):

                def edge_of(i):
                    turn = (2 * LANES - 2 - 4 * place(slot, r, i)) % LANES
                    return pltpu.roll(packed, turn, 1)

                edge_total = edge_of(0)
                for i in range(1, n_half):
                    edge_total = edge_total + edge_of(i)
                prepare(
                    slot, base + r,
                    lambda i: rows_in[side, place(slot, r, i)].astype(F32),
                    edge_of, edge_total,
                )

    def lag_group(slot, start):
        @pl.loop(0, CH)
        def _(n):
            r = lax.rem(start + n, rows)
            sums = [None] * 25
            for i in range(n_half):
                centre = spread[slot, r + REACH, i, REACH]
                for k in range(25):
                    term = centre * spread[slot, r + k // 5, i, k % 5]
                    sums[k] = term if i == 0 else sums[k] + term
            for k in range(25):
                reduced[k, pl.ds(pl.multiple_of(n * 8, 8), 8), :] = sums[k]

    def lag_plane(k):
        total = reduced[k, pl.ds(0, CH, stride=8), :]
        for n in range(1, 8):
            total = total + reduced[k, pl.ds(n, CH, stride=8), :]
        return total * inverse

    def pack_planes(at):
        for p in range(13):
            sent[at, p] = lag_plane(12 + p)
        side = zero
        for k in range(12):
            plane = lag_plane(k)
            if k % 5 != REACH:
                side = jnp.where(group == k, pltpu.roll(plane, 4 * k + 2, 1), side)
            if at is WRAP:
                sent[at + 1, k] = plane
        sent[at, 13] = side

    def mean_rows(c):
        return pl.ds(pl.multiple_of(8 + c * CH, CH), CH)

    def send_group(at, c):
        lag_group(0, c * CH + REACH)
        pack_planes(at)
        for kind in range(2):
            sent[at, 14 + kind] = means[0, kind, mean_rows(c), :]
        to_partner(at, 1).start()

    def send_wrap():
        lag_group(0, rows - CH + REACH)
        pack_planes(WRAP)
        for kind in range(2):
            sent[WRAP, 14 + kind] = means[0, kind, mean_rows(0), :]
            sent[WRAP + 1, 12 + kind] = means[0, kind, mean_rows(chunks - 1), :]
            sent[WRAP + 1, 14 + kind] = (
                means[0, kind, pl.ds(0, 8), :] + means[0, kind, pl.ds(8 + rows, 8), :]
            )
        to_partner(WRAP, 2).start()

    def add(k, at, value, keep=None):
        if keep is not None:
            value = jnp.where(keep, value, 0.0)
        totals[k, pl.ds(at, 8), :] += value

    wrapped = ((rows - CH + REACH, sub < CH - REACH), (REACH - CH, sub >= CH - REACH))

    def own_group(c):
        lag_group(1, c * CH + REACH)
        for k in range(25):
            add(k, 8 + c * CH + REACH, lag_plane(k))

    def own_wrap():
        lag_group(1, rows - CH + REACH)
        for k in range(25):
            plane = lag_plane(k)
            for start, keep in wrapped:
                add(k, 8 + start, plane, keep)

    def add_far(at, base, keep=None):
        gap = {}
        for a in range(-REACH, REACH + 1):
            value, edge = (
                means[1, kind, pl.ds(base + a, 8), :] - far_means[kind, pl.ds(base + a, 8), :]
                for kind in range(2)
            )
            for b in range(-REACH, REACH + 1):
                gap[a, b] = shifted(value, edge, b)
        centre = gap[0, 0] * 0.25
        side = got[at, 13]
        for k in range(25):
            a, b = k // 5 - REACH, k % 5 - REACH
            value = centre * gap[a, b]
            if k >= 12:
                plane = got[at, k - 12]
                value = value + plane
                if k > 12:
                    moved = pltpu.roll(plane, b % LANES, 1)
                    inside = (lane >= b) & (lane < LANES + b)
                    add(24 - k, base + a, jnp.where(inside, moved, 0.0), keep)
            else:
                if b != 0:
                    column = pltpu.roll(side, (2 * LANES - 4 * k - 2) % LANES, 1)
                    outside = (lane < -b) | (lane >= LANES - b)
                    if keep is not None:
                        outside = outside & (sub != 6 if a == -1 else sub < 6) if a < 0 else outside
                    value = value + jnp.where(outside, column, 0.0)
                if keep is not None and a < 0:
                    direct = sub == 6 if a == -1 else sub >= 6
                    value = value + jnp.where(direct, got[at + 1, k], 0.0)
            add(k, base, value, keep)

    def take_group(at, c):
        to_partner(at, 1).wait_recv()
        for kind in range(2):
            far_means[kind, mean_rows(c), :] = got[at, 14 + kind]
        add_far(at, 8 + c * CH + REACH)

    def take_wrap():
        to_partner(WRAP, 2).wait_recv()
        for kind in range(2):
            far_means[kind, mean_rows(0), :] = got[WRAP, 14 + kind]
            far_means[kind, mean_rows(chunks - 1), :] = got[WRAP + 1, 12 + kind]
            ends = got[WRAP + 1, 14 + kind]
            far_means[kind, pl.ds(0, 8), :] = jnp.where(sub >= 8 - REACH, ends, 0.0)
            far_means[kind, pl.ds(8 + rows, 8), :] = jnp.where(sub < REACH, ends, 0.0)
        for start, keep in wrapped:
            add_far(WRAP, 8 + start, keep)

    take_chunk(0)
    give_rows(0, 0, 0)

    @pl.when(has_above)
    def _():
        row_copy(0, above).start()

    take_chunk(1)
    give_rows(1, chunks - 1, CH - REACH)

    @pl.when(has_below)
    def _():
        row_copy(1, below).start()

    @pl.loop(2, chunks - 1)
    def _(step):
        c = chunk_at(step)
        take_chunk(step)

        @pl.when(step == 3)
        def _():
            empty = jnp.zeros((2, REACH, n_half, 5, 8, LANES), F32)

            @pl.when(has_below)
            def _():
                row_copy(0, below).wait_recv()
                take_rows(0, rows)

            @pl.when(jnp.logical_not(has_below))
            def _():
                spread[:, rows + REACH : rows + 2 * REACH] = empty

            @pl.when(has_above)
            def _():
                row_copy(1, above).wait_recv()
                take_rows(1, -REACH)

            @pl.when(jnp.logical_not(has_above))
            def _():
                spread[:, 0:REACH] = empty

            send_wrap()

        send_group(step, c)
        own_group(c)

        @pl.when(step == 3)
        def _():
            own_wrap()

    last = chunks - 1
    take_chunk(last)
    send_group(last, 1)
    send_group(last + 1, 0)
    own_group(1)
    own_group(0)
    take_wrap()

    @pl.loop(2, last)
    def _(step):
        take_group(step, chunk_at(step))

    take_group(last, 1)
    take_group(last + 1, 0)
    out[...] = totals[:, 8 : 8 + rows, :]

    all_of(block.at[:, :, pl.ds(0, n_half - 1)], send_sem, recv_sem.at[0]).wait_send()
    all_of(edges_in.at[:, pl.ds(0, n_half - 1)], edge_send, edge_recv).wait_send()
    to_partner(0, chunks + 1).wait_send()

    @pl.when(has_above)
    def _():
        row_copy(0, above).wait_send()

    @pl.when(has_below)
    def _():
        row_copy(1, below).wait_send()


def body(movie):
    frames, rows, width = movie.shape
    n_frame, n_strip = lax.axis_size("frame"), lax.axis_size("strip")
    chunks, n_half = rows // CH, n_frame // 2
    kernel = functools.partial(lag_kernel, n_frame, n_strip, 4, frames * n_frame)
    DMA = pltpu.SemaphoreType.DMA
    padded = rows + 16
    return pl.pallas_call(
        kernel,
        out_shape=jax.ShapeDtypeStruct((25, rows, width // n_frame), F32),
        in_specs=[pl.BlockSpec(memory_space=pl.ANY)],
        out_specs=pl.BlockSpec(memory_space=pltpu.VMEM),
        scratch_shapes=[
            pltpu.VMEM((chunks, 2, n_half, frames, CH, LANES), BF16),
            pltpu.VMEM((2, n_half, rows // 32, 8, LANES), BF16),
            pltpu.VMEM((n_frame, rows // 32, 8, LANES), BF16),
            pltpu.VMEM((2, 2 * REACH * n_half + 1, 8, LANES), BF16),
            pltpu.VMEM((2, 2 * REACH * n_half + 1, 8, LANES), BF16),
            pltpu.VMEM((frames, rows, width), BF16),
            pltpu.VMEM((2, rows + 2 * REACH, n_half, 5, 8, LANES), F32),
            pltpu.VMEM((frames * rows, LANES), F32),
            pltpu.VMEM((n_frame * CH * 8, LANES), F32),
            pltpu.VMEM((25, CH * 8, LANES), F32),
            pltpu.VMEM((chunks + 1, 16, 8, LANES), F32),
            pltpu.VMEM((chunks + 1, 16, 8, LANES), F32),
            pltpu.VMEM((2, 2, padded, LANES), F32),
            pltpu.VMEM((2, padded, LANES), F32),
            pltpu.VMEM((25, padded, LANES), F32),
            DMA, DMA((chunks,)), DMA, DMA, DMA, DMA, DMA((2,)), DMA((2,)),
            DMA, DMA((chunks + 1,)),
        ],
        compiler_params=pltpu.CompilerParams(
            collective_id=0, has_side_effects=True, vmem_limit_bytes=56 * 2**20
        ),
        name="lag_maps",
    )(movie)


def solution(mesh):
    return jax.shard_map(
        body,
        mesh=mesh,
        in_specs=(P("frame", "strip", None),),
        out_specs=P(None, "strip", "frame"),
        check_vma=False,
    )
```

```python
import functools

import jax
import jax.numpy as jnp
from jax import lax
from jax.experimental import pallas as pl
from jax.experimental.pallas import tpu as pltpu
from jax.sharding import PartitionSpec as P

MESH = pl.DeviceIdType.MESH
LANES = 128
CH = 8
REACH = 2
AHEAD = 3
F32 = jnp.float32
BF16 = jnp.bfloat16


def lag_kernel(
    n_frame, n_strip, n_x, frames_total,
    movie, out,
    block, edges_in, edges_out, rows_in, rows_out, held, spread, picked, work,
    reduced, sent, got, means, far_means, totals,
    send_sem, recv_sem, own_sem, held_sem, edge_send, edge_recv, row_send, row_recv,
    part_send, part_recv,
):
    frames, rows, width = movie.shape
    chunks = rows // CH
    n_half = n_frame // 2
    me = lax.axis_index("frame")
    strip = lax.axis_index("strip")
    first = (me // n_half) * n_half
    mine = me - first
    partner = lax.rem(me + n_half, n_frame)
    inverse = 1.0 / frames_total

    lane = lax.broadcasted_iota(jnp.int32, (8, LANES), 1)
    sub = lax.broadcasted_iota(jnp.int32, (8, LANES), 0)
    group = lane // 4
    zero = jnp.zeros((8, LANES), F32)

    def peer(k):
        dx, dz = k // 2, lax.rem(k, 2)
        return lax.rem(mine // n_x + dz, 2) * n_x + lax.rem(lax.rem(mine, n_x) + dx, n_x)

    def chunk_at(step):
        return lax.rem(chunks - step, chunks)

    def owner(slot, index):
        return lax.rem(first + index + (1 - slot) * n_half, n_frame)

    def tile(c, g):
        return movie.at[
            :, pl.ds(pl.multiple_of(c * CH, CH), CH),
            pl.ds(pl.multiple_of(g * LANES, LANES), LANES),
        ]

    def own_copy(c, slot):
        return pltpu.make_async_copy(tile(c, owner(slot, mine)), block.at[c, slot, mine], own_sem)

    def to_peer(src, dst, send, recv, index):
        return pltpu.make_async_remote_copy(
            src_ref=src, dst_ref=dst, send_sem=send, recv_sem=recv,
            device_id={"frame": first + index}, device_id_type=MESH,
        )

    def all_of(ref, send, recv):
        return to_peer(ref, ref, send, recv, peer(1))

    def to_partner(m, count):
        at = 16 * m
        return pltpu.make_async_remote_copy(
            src_ref=sent.at[pl.ds(at, count)], dst_ref=got.at[pl.ds(at, count)],
            send_sem=part_send, recv_sem=part_recv.at[m],
            device_id={"frame": partner}, device_id_type=MESH,
        )

    def row_copy(side, to):
        return pltpu.make_async_remote_copy(
            src_ref=rows_out.at[side], dst_ref=rows_in.at[side],
            send_sem=row_send.at[side], recv_sem=row_recv.at[side],
            device_id={"strip": to}, device_id_type=MESH,
        )

    above, below = jnp.maximum(strip - 1, 0), jnp.minimum(strip + 1, n_strip - 1)
    has_above, has_below = strip > 0, strip < n_strip - 1

    whole = pltpu.make_async_copy(movie, held, held_sem)
    whole.start()

    @pl.loop(0, chunks)
    def _(c):
        own_copy(c, 0).start()
        own_copy(c, 1).start()

    barrier = pltpu.get_barrier_semaphore()

    @pl.loop(1, n_half)
    def _(k):
        pl.semaphore_signal(
            barrier, inc=1, device_id={"frame": first + peer(k)}, device_id_type=MESH
        )

    pl.semaphore_signal(barrier, inc=1, device_id={"frame": partner}, device_id_type=MESH)

    @pl.when(has_above)
    def _():
        pl.semaphore_signal(barrier, inc=1, device_id={"strip": above}, device_id_type=MESH)

    @pl.when(has_below)
    def _():
        pl.semaphore_signal(barrier, inc=1, device_id={"strip": below}, device_id_type=MESH)

    totals[...] = jnp.zeros(totals.shape, F32)
    means[...] = jnp.zeros(means.shape, F32)

    whole.wait()
    pick_row = lax.broadcasted_iota(jnp.int32, (width, LANES), 0)
    pick_lane = lax.broadcasted_iota(jnp.int32, (width, LANES), 1)
    j = lax.rem(pick_lane, 4)
    target = (pick_lane // 4) * LANES + jnp.where(j < 2, j - 2, LANES - 2 + j)
    pick = jnp.where((pick_row == target) & (pick_lane < 4 * n_frame), 1.0, 0.0).astype(BF16)
    for f in range(frames):
        picked[pl.ds(f * rows, rows), :] = jnp.dot(held[f], pick, preferred_element_type=F32)

    @pl.loop(0, rows, unroll=8)
    def _(r):
        v = picked[pl.ds(r, frames, stride=rows), :]
        work[pl.ds(pl.multiple_of(r * 8, 8), 8), :] = pltpu.roll(v, 4 * lax.rem(r, 32), 1)

    @pl.loop(0, n_frame)
    def _(g):
        for q in range(rows // 32):
            packed = zero
            for r in range(32):
                v = work[pl.ds((q * 32 + r) * 8, 8), :]
                packed = jnp.where(group == lax.rem(r + g, 32), v, packed)
            edges_out[g, q] = pltpu.roll(packed, lax.rem(LANES - 4 * g, LANES), 1).astype(BF16)

    neighbours = jnp.where(has_above, 1, 0) + jnp.where(has_below, 1, 0)
    pl.semaphore_wait(barrier, n_half + neighbours)

    def send_chunk(step):
        c = chunk_at(step)

        @pl.loop(1, n_half)
        def _(k):
            p = peer(k)
            for slot in range(2):
                to_peer(
                    tile(c, owner(slot, p)), block.at[c, slot, mine],
                    send_sem, recv_sem.at[c], p,
                ).start()

    @pl.loop(1, n_half)
    def _(k):
        p = peer(k)
        for slot in range(2):
            to_peer(
                edges_out.at[owner(slot, p)], edges_in.at[slot, mine], edge_send, edge_recv, p
            ).start()

    for step in range(AHEAD):
        send_chunk(step)
    for slot in range(2):
        edges_in[slot, mine] = edges_out[owner(slot, mine)]

    @pl.loop(0, chunks)
    def _(c):
        own_copy(c, 0).wait()
        own_copy(c, 1).wait()

    beside = []
    for slot in range(2):
        g = owner(slot, mine)
        beside.append(((lane >= LANES - 2) & (g > 0)) | ((lane < 2) & (g < n_frame - 1)))

    def shifted(value, edge, b):
        if b == 0:
            return value
        near = lane < b if b > 0 else lane >= LANES + b
        return pltpu.roll(jnp.where(near, edge, value), (LANES - b) % LANES, 1)

    def over_frames(total):
        return jnp.sum(total, axis=0, keepdims=True) * (1.0 / (n_half * frames))

    def prepare(slot, r, row_of, edge_of, edge_total):
        total = row_of(0)
        for i in range(1, n_half):
            total = total + row_of(i)
        mean, edge_mean = over_frames(total), over_frames(edge_total)
        means[slot, 0, pl.ds(r + 8, 1), :] = mean
        means[slot, 1, pl.ds(r + 8, 1), :] = jnp.where(beside[slot][:1], edge_mean, 0.0)
        for i in range(n_half):
            value = row_of(i) - mean
            edge = jnp.where(beside[slot], edge_of(i) - edge_mean, 0.0)
            for b in range(-REACH, REACH + 1):
                spread[slot, r + REACH, i, b + REACH] = shifted(value, edge, b)

    def work_row(slot, i, r):
        return work[pl.ds((slot * n_half + i) * CH * 8 + r, 8, stride=CH), :]

    def edge_turn(c, r):
        return lax.rem(2 * LANES - 2 - 4 * (lax.rem(c, 32 // CH) * CH + r), LANES)

    def edge_tile(slot, i, c):
        return edges_in[slot, i, c // (32 // CH)].astype(F32)

    def take_chunk(step):
        c = chunk_at(step)
        all_of(block.at[c, :, pl.ds(0, n_half - 1)], send_sem, recv_sem.at[c]).wait_recv()

        @pl.when(step + AHEAD < chunks)
        def _():
            send_chunk(step + AHEAD)

        for slot in range(2):
            for i in range(n_half):
                work[pl.ds((slot * n_half + i) * CH * 8, CH * 8), :] = (
                    block[c, slot, i].astype(F32).reshape(CH * 8, LANES)
                )

        @pl.when(step == 0)
        def _():
            all_of(edges_in.at[:, pl.ds(0, n_half - 1)], edge_send, edge_recv).wait_recv()

        edge_totals = []
        for slot in range(2):
            edge_total = edge_tile(slot, 0, c)
            for i in range(1, n_half):
                edge_total = edge_total + edge_tile(slot, i, c)
            edge_totals.append(edge_total)

        @pl.loop(0, CH, unroll=2)
        def _(r):
            turn = edge_turn(c, r)
            for slot in range(2):
                prepare(
                    slot, c * CH + r,
                    lambda i: work_row(slot, i, r),
                    lambda i: pltpu.roll(edge_tile(slot, i, c), turn, 1),
                    pltpu.roll(edge_totals[slot], turn, 1),
                )

    def place(slot, r, i):
        return (slot * REACH + r) * n_half + i

    def give_rows(side, c, start):
        packed = zero
        for slot in range(2):
            for r in range(REACH):
                for i in range(n_half):
                    at = place(slot, r, i)
                    rows_out[side, at] = work_row(slot, i, start + r).astype(BF16)
                    turn = lax.rem(edge_turn(c, start + r) + 2 + 4 * at, LANES)
                    packed = jnp.where(
                        group == at, pltpu.roll(edge_tile(slot, i, c), turn, 1), packed
                    )
        rows_out[side, 2 * REACH * n_half] = packed.astype(BF16)

    def take_rows(side, base):
        packed = rows_in[side, 2 * REACH * n_half].astype(F32)
        for slot in range(2):
            for r in range(REACH):

                def edge_of(i):
                    turn = (2 * LANES - 2 - 4 * place(slot, r, i)) % LANES
                    return pltpu.roll(packed, turn, 1)

                edge_total = edge_of(0)
                for i in range(1, n_half):
                    edge_total = edge_total + edge_of(i)
                prepare(
                    slot, base + r,
                    lambda i: rows_in[side, place(slot, r, i)].astype(F32),
                    edge_of, edge_total,
                )

    def lag_group(slot, row_at):
        @pl.loop(0, CH)
        def _(n):
            r = row_at(n)
            sums = [None] * 25
            for i in range(n_half):
                centre = spread[slot, r + REACH, i, REACH]
                for k in range(25):
                    term = centre * spread[slot, r + k // 5, i, k % 5]
                    sums[k] = term if i == 0 else sums[k] + term
            for k in range(25):
                reduced[k, pl.ds(pl.multiple_of(n * 8, 8), 8), :] = sums[k]

    def lag_plane(k):
        total = reduced[k, pl.ds(0, CH, stride=8), :]
        for n in range(1, 8):
            total = total + reduced[k, pl.ds(n, CH, stride=8), :]
        return total * inverse

    def mean_rows(c):
        return pl.ds(pl.multiple_of(8 + c * CH, CH), CH)

    def put(value, g):
        return pltpu.roll(value, (4 * g + 2) % LANES, 1)

    def unput(value, g):
        return pltpu.roll(value, (2 * LANES - 4 * g - 2) % LANES, 1)

    def plain(c):
        start = c * CH + REACH
        return (lambda n: start + n), ((start, None),)

    def inner_ends():
        return (
            lambda n: jnp.where(n < 4, rows - CH + REACH + n, n - REACH),
            ((rows - CH + REACH, sub < 4), (-REACH, sub >= 4)),
        )

    def outer_ends():
        return (
            lambda n: jnp.where(n < 4, CH - REACH + n, lax.rem(rows - CH + REACH + n, rows)),
            (
                (CH - REACH, sub < 4),
                (rows - CH + REACH, (sub >= 4) & (sub < 6)),
                (REACH - CH, sub >= 6),
            ),
        )

    def send_group(m, row_at, chunk_means, ends=False):
        at = 16 * m
        lag_group(0, row_at)
        for p in range(13):
            sent[at + p] = lag_plane(12 + p)
        side, low = zero, [zero] * 3
        for k in range(12):
            if k % 5 == REACH and not ends:
                continue
            plane = lag_plane(k)
            if k % 5 != REACH:
                side = jnp.where(group == k, put(plane, k), side)
            if ends:
                place = 2 * (k % 4)
                low[k // 4] = jnp.where(
                    sub // 2 == k % 4, pltpu.roll(plane, (place + 2) % 8, 0), low[k // 4]
                )
        for n, (mean, edge) in enumerate(chunk_means):
            sent[at + 14 + n] = mean
            side = jnp.where(group == 12 + n, put(edge, 12 + n), side)
        sent[at + 13] = side
        if ends:
            for n in range(3):
                sent[at + 15 + n] = low[n]
        to_partner(m, planes(len(chunk_means), ends)).start()

    def planes(n_means, ends=False):
        return 14 + n_means + (3 if ends else 0)

    def chunk_mean(c):
        return tuple(means[0, kind, mean_rows(c), :] for kind in range(2))

    def add(k, at, value, keep=None):
        if keep is not None:
            value = jnp.where(keep, value, 0.0)
        totals[k, pl.ds(at, 8), :] += value

    def own_group(row_at, parts):
        lag_group(1, row_at)
        for k in range(25):
            plane = lag_plane(k)
            for start, keep in parts:
                add(k, 8 + start, plane, keep)

    def add_far(m, base, keep, ends):
        at = 16 * m
        gap = {}
        for a in range(-REACH, REACH + 1):
            value, edge = (
                means[1, kind, pl.ds(base + a, 8), :] - far_means[kind, pl.ds(base + a, 8), :]
                for kind in range(2)
            )
            for b in range(-REACH, REACH + 1):
                gap[a, b] = shifted(value, edge, b)
        centre = gap[0, 0] * 0.25
        side = got[at + 13]
        for k in range(25):
            a, b = k // 5 - REACH, k % 5 - REACH
            value = centre * gap[a, b]
            if k >= 12:
                plane = got[at + k - 12]
                value = value + plane
                if k > 12:
                    moved = pltpu.roll(plane, b % LANES, 1)
                    inside = (lane >= b) & (lane < LANES + b)
                    add(24 - k, base + a, jnp.where(inside, moved, 0.0), keep)
            else:
                direct = None
                if ends and a < 0:
                    direct = sub == 6 if a == -1 else sub >= 6
                if b != 0:
                    outside = (lane < -b) | (lane >= LANES - b)
                    if direct is not None:
                        outside = outside & jnp.logical_not(direct)
                    value = value + jnp.where(outside, unput(side, k), 0.0)
                if direct is not None:
                    low = pltpu.roll(got[at + 15 + k // 4], 6 - 2 * (k % 4), 0)
                    value = value + jnp.where(direct, low, 0.0)
            add(k, base, value, keep)

    def take_means(m, n, where):
        far_means[0, where, :] = got[16 * m + 14 + n]
        far_means[1, where, :] = unput(got[16 * m + 13], 12 + n)

    def take_group(m, parts, ends=False):
        for start, keep in parts:
            add_far(m, 8 + start, keep, ends)

    take_chunk(0)
    give_rows(0, 0, 0)

    @pl.when(has_above)
    def _():
        row_copy(0, above).start()

    take_chunk(1)
    give_rows(1, chunks - 1, CH - REACH)

    @pl.when(has_below)
    def _():
        row_copy(1, below).start()

    send_group(0, inner_ends()[0], (chunk_mean(chunks - 1), chunk_mean(0)))
    own_group(*inner_ends())

    @pl.loop(2, chunks - 1)
    def _(step):
        c = chunk_at(step)
        take_chunk(step)

        @pl.when(step == 4)
        def _():
            empty = jnp.zeros((2, REACH, n_half, 5, 8, LANES), F32)

            @pl.when(has_below)
            def _():
                row_copy(0, below).wait_recv()
                take_rows(0, rows)

            @pl.when(jnp.logical_not(has_below))
            def _():
                spread[:, rows + REACH : rows + 2 * REACH] = empty

            @pl.when(has_above)
            def _():
                row_copy(1, above).wait_recv()
                take_rows(1, -REACH)

            @pl.when(jnp.logical_not(has_above))
            def _():
                spread[:, 0:REACH] = empty

        send_group(step - 1, plain(c)[0], (chunk_mean(c),))
        own_group(*plain(c))

    last = chunks - 1
    take_chunk(last)
    send_group(last - 1, plain(1)[0], (chunk_mean(1),))
    beyond = tuple(
        means[0, kind, pl.ds(0, 8), :] + means[0, kind, pl.ds(8 + rows, 8), :] for kind in range(2)
    )
    send_group(last, outer_ends()[0], (beyond,), ends=True)
    own_group(*plain(1))
    own_group(*outer_ends())

    to_partner(0, planes(2)).wait_recv()
    take_means(0, 0, mean_rows(chunks - 1))
    take_means(0, 1, mean_rows(0))
    take_group(0, inner_ends()[1])

    @pl.loop(2, chunks)
    def _(step):
        c = chunk_at(step)
        to_partner(step - 1, planes(1)).wait_recv()
        take_means(step - 1, 0, mean_rows(c))
        take_group(step - 1, plain(c)[1])

    to_partner(last, planes(1, True)).wait_recv()
    ends = (got[16 * last + 14], unput(got[16 * last + 13], 12))
    for kind in range(2):
        far_means[kind, pl.ds(0, 8), :] = jnp.where(sub >= 8 - REACH, ends[kind], 0.0)
        far_means[kind, pl.ds(8 + rows, 8), :] = jnp.where(sub < REACH, ends[kind], 0.0)
    take_group(last, outer_ends()[1], ends=True)
    out[...] = totals[:, 8 : 8 + rows, :]

    all_of(block.at[:, :, pl.ds(0, n_half - 1)], send_sem, recv_sem.at[0]).wait_send()
    all_of(edges_in.at[:, pl.ds(0, n_half - 1)], edge_send, edge_recv).wait_send()
    every = sent.at[pl.ds(0, planes(2) + (chunks - 2) * planes(1) + planes(1, True))]
    all_of(every, part_send, part_recv.at[0]).wait_send()

    @pl.when(has_above)
    def _():
        row_copy(0, above).wait_send()

    @pl.when(has_below)
    def _():
        row_copy(1, below).wait_send()


def body(movie):
    frames, rows, width = movie.shape
    n_frame, n_strip = lax.axis_size("frame"), lax.axis_size("strip")
    chunks, n_half = rows // CH, n_frame // 2
    kernel = functools.partial(lag_kernel, n_frame, n_strip, 4, frames * n_frame)
    DMA = pltpu.SemaphoreType.DMA
    padded = rows + 16
    return pl.pallas_call(
        kernel,
        out_shape=jax.ShapeDtypeStruct((25, rows, width // n_frame), F32),
        in_specs=[pl.BlockSpec(memory_space=pl.ANY)],
        out_specs=pl.BlockSpec(memory_space=pltpu.VMEM),
        scratch_shapes=[
            pltpu.VMEM((chunks, 2, n_half, frames, CH, LANES), BF16),
            pltpu.VMEM((2, n_half, rows // 32, 8, LANES), BF16),
            pltpu.VMEM((n_frame, rows // 32, 8, LANES), BF16),
            pltpu.VMEM((2, 2 * REACH * n_half + 1, 8, LANES), BF16),
            pltpu.VMEM((2, 2 * REACH * n_half + 1, 8, LANES), BF16),
            pltpu.VMEM((frames, rows, width), BF16),
            pltpu.VMEM((2, rows + 2 * REACH, n_half, 5, 8, LANES), F32),
            pltpu.VMEM((frames * rows, LANES), F32),
            pltpu.VMEM((n_frame * CH * 8, LANES), F32),
            pltpu.VMEM((25, CH * 8, LANES), F32),
            pltpu.VMEM((16 * chunks + 2, 8, LANES), F32),
            pltpu.VMEM((16 * chunks + 2, 8, LANES), F32),
            pltpu.VMEM((2, 2, padded, LANES), F32),
            pltpu.VMEM((2, padded, LANES), F32),
            pltpu.VMEM((25, padded, LANES), F32),
            DMA, DMA((chunks,)), DMA, DMA, DMA, DMA, DMA((2,)), DMA((2,)),
            DMA, DMA((chunks,)),
        ],
        compiler_params=pltpu.CompilerParams(
            collective_id=0, has_side_effects=True, vmem_limit_bytes=56 * 2**20
        ),
        name="lag_maps",
    )(movie)


def solution(mesh):
    return jax.shard_map(
        body,
        mesh=mesh,
        in_specs=(P("frame", "strip", None),),
        out_specs=P(None, "strip", "frame"),
        check_vma=False,
    )
```

```python
import functools

import jax
import jax.numpy as jnp
from jax import lax
from jax.experimental import pallas as pl
from jax.experimental.pallas import tpu as pltpu
from jax.sharding import PartitionSpec as P

MESH = pl.DeviceIdType.MESH
LANES = 128
CH = 8
REACH = 2
AHEAD = 3
F32 = jnp.float32
BF16 = jnp.bfloat16


def lag_kernel(
    n_frame, n_strip, n_x, frames_total,
    movie, out,
    block, edges_in, edges_out, rows_in, rows_out, held, spread, picked, work,
    reduced, sent, got, means, far_means, totals,
    send_sem, recv_sem, own_sem, held_sem, edge_send, edge_recv, row_send, row_recv,
    part_send, part_recv,
):
    frames, rows, width = movie.shape
    chunks = rows // CH
    n_half = n_frame // 2
    me = lax.axis_index("frame")
    strip = lax.axis_index("strip")
    first = (me // n_half) * n_half
    mine = me - first
    partner = lax.rem(me + n_half, n_frame)
    inverse = 1.0 / frames_total

    lane = lax.broadcasted_iota(jnp.int32, (8, LANES), 1)
    sub = lax.broadcasted_iota(jnp.int32, (8, LANES), 0)
    group = lane // 4
    zero = jnp.zeros((8, LANES), F32)

    def peer(k):
        dx, dz = k // 2, lax.rem(k, 2)
        return lax.rem(mine // n_x + dz, 2) * n_x + lax.rem(lax.rem(mine, n_x) + dx, n_x)

    def chunk_at(step):
        return lax.rem(chunks - step, chunks)

    def owner(slot, index):
        return lax.rem(first + index + (1 - slot) * n_half, n_frame)

    def tile(c, g):
        return movie.at[
            :, pl.ds(pl.multiple_of(c * CH, CH), CH),
            pl.ds(pl.multiple_of(g * LANES, LANES), LANES),
        ]

    def own_copy(c, slot):
        return pltpu.make_async_copy(tile(c, owner(slot, mine)), block.at[c, slot, mine], own_sem)

    def to_peer(src, dst, send, recv, index):
        return pltpu.make_async_remote_copy(
            src_ref=src, dst_ref=dst, send_sem=send, recv_sem=recv,
            device_id={"frame": first + index}, device_id_type=MESH,
        )

    def all_of(ref, send, recv):
        return to_peer(ref, ref, send, recv, peer(1))

    def to_partner(m, count):
        at = 16 * m
        return pltpu.make_async_remote_copy(
            src_ref=sent.at[pl.ds(at, count)], dst_ref=got.at[pl.ds(at, count)],
            send_sem=part_send, recv_sem=part_recv.at[m],
            device_id={"frame": partner}, device_id_type=MESH,
        )

    def row_copy(side, to):
        return pltpu.make_async_remote_copy(
            src_ref=rows_out.at[side], dst_ref=rows_in.at[side],
            send_sem=row_send.at[side], recv_sem=row_recv.at[side],
            device_id={"strip": to}, device_id_type=MESH,
        )

    above, below = jnp.maximum(strip - 1, 0), jnp.minimum(strip + 1, n_strip - 1)
    has_above, has_below = strip > 0, strip < n_strip - 1

    barrier = pltpu.get_barrier_semaphore()

    @pl.when(has_above)
    def _():
        pl.semaphore_signal(barrier, inc=1, device_id={"strip": above}, device_id_type=MESH)

    @pl.when(has_below)
    def _():
        pl.semaphore_signal(barrier, inc=1, device_id={"strip": below}, device_id_type=MESH)

    @pl.loop(1, n_half)
    def _(k):
        pl.semaphore_signal(
            barrier, inc=1, device_id={"frame": first + peer(k)}, device_id_type=MESH
        )

    pl.semaphore_signal(barrier, inc=1, device_id={"frame": partner}, device_id_type=MESH)

    whole = pltpu.make_async_copy(movie, held, held_sem)
    whole.start()

    @pl.loop(0, chunks)
    def _(c):
        own_copy(c, 0).start()
        own_copy(c, 1).start()

    totals[...] = jnp.zeros(totals.shape, F32)
    means[...] = jnp.zeros(means.shape, F32)

    whole.wait()
    pick_row = lax.broadcasted_iota(jnp.int32, (width, LANES), 0)
    pick_lane = lax.broadcasted_iota(jnp.int32, (width, LANES), 1)
    j = lax.rem(pick_lane, 4)
    target = (pick_lane // 4) * LANES + jnp.where(j < 2, j - 2, LANES - 2 + j)
    pick = jnp.where((pick_row == target) & (pick_lane < 4 * n_frame), 1.0, 0.0).astype(BF16)
    for f in range(frames):
        picked[pl.ds(f * rows, rows), :] = jnp.dot(held[f], pick, preferred_element_type=F32)

    @pl.loop(0, rows, unroll=8)
    def _(r):
        v = picked[pl.ds(r, frames, stride=rows), :]
        work[pl.ds(pl.multiple_of(r * 8, 8), 8), :] = pltpu.roll(v, 4 * lax.rem(r, 32), 1)

    @pl.loop(0, n_frame)
    def _(g):
        for q in range(rows // 32):
            packed = zero
            for r in range(32):
                v = work[pl.ds((q * 32 + r) * 8, 8), :]
                packed = jnp.where(group == lax.rem(r + g, 32), v, packed)
            edges_out[g, q] = pltpu.roll(packed, lax.rem(LANES - 4 * g, LANES), 1).astype(BF16)

    neighbours = jnp.where(has_above, 1, 0) + jnp.where(has_below, 1, 0)
    pl.semaphore_wait(barrier, n_half + neighbours)

    def send_chunk(step):
        c = chunk_at(step)

        @pl.loop(1, n_half)
        def _(k):
            p = peer(k)
            for slot in range(2):
                to_peer(
                    tile(c, owner(slot, p)), block.at[c, slot, mine],
                    send_sem, recv_sem.at[c], p,
                ).start()

    @pl.loop(1, n_half)
    def _(k):
        p = peer(k)
        for slot in range(2):
            to_peer(
                edges_out.at[owner(slot, p)], edges_in.at[slot, mine], edge_send, edge_recv, p
            ).start()

    for step in range(AHEAD):
        send_chunk(step)
    for slot in range(2):
        edges_in[slot, mine] = edges_out[owner(slot, mine)]

    @pl.loop(0, chunks)
    def _(c):
        own_copy(c, 0).wait()
        own_copy(c, 1).wait()

    beside = []
    for slot in range(2):
        g = owner(slot, mine)
        beside.append(((lane >= LANES - 2) & (g > 0)) | ((lane < 2) & (g < n_frame - 1)))

    def shifted(value, edge, b):
        if b == 0:
            return value
        near = lane < b if b > 0 else lane >= LANES + b
        return pltpu.roll(jnp.where(near, edge, value), (LANES - b) % LANES, 1)

    def over_frames(total):
        return jnp.sum(total, axis=0, keepdims=True) * (1.0 / (n_half * frames))

    def prepare(slot, r, row_of, edge_of, edge_total):
        total = row_of(0)
        for i in range(1, n_half):
            total = total + row_of(i)
        mean, edge_mean = over_frames(total), over_frames(edge_total)
        means[slot, 0, pl.ds(r + 8, 1), :] = mean
        means[slot, 1, pl.ds(r + 8, 1), :] = jnp.where(beside[slot][:1], edge_mean, 0.0)
        for i in range(n_half):
            value = row_of(i) - mean
            edge = jnp.where(beside[slot], edge_of(i) - edge_mean, 0.0)
            for b in range(-REACH, REACH + 1):
                spread[slot, r + REACH, i, b + REACH] = shifted(value, edge, b)

    def work_row(slot, i, r):
        return work[pl.ds((slot * n_half + i) * CH * 8 + r, 8, stride=CH), :]

    def edge_turn(c, r):
        return lax.rem(2 * LANES - 2 - 4 * (lax.rem(c, 32 // CH) * CH + r), LANES)

    def edge_tile(slot, i, c):
        return edges_in[slot, i, c // (32 // CH)].astype(F32)

    def take_chunk(step):
        c = chunk_at(step)
        all_of(block.at[c, :, pl.ds(0, n_half - 1)], send_sem, recv_sem.at[c]).wait_recv()

        @pl.when(step + AHEAD < chunks)
        def _():
            send_chunk(step + AHEAD)

        for slot in range(2):
            for i in range(n_half):
                work[pl.ds((slot * n_half + i) * CH * 8, CH * 8), :] = (
                    block[c, slot, i].astype(F32).reshape(CH * 8, LANES)
                )

        @pl.when(step == 0)
        def _():
            all_of(edges_in.at[:, pl.ds(0, n_half - 1)], edge_send, edge_recv).wait_recv()

        prepare_chunk(0, c)

    def prepare_chunk(slot, c):
        edge_total = edge_tile(slot, 0, c)
        for i in range(1, n_half):
            edge_total = edge_total + edge_tile(slot, i, c)

        @pl.loop(0, CH, unroll=4)
        def _(r):
            turn = edge_turn(c, r)
            prepare(
                slot, c * CH + r,
                lambda i: work_row(slot, i, r),
                lambda i: pltpu.roll(edge_tile(slot, i, c), turn, 1),
                pltpu.roll(edge_total, turn, 1),
            )

    def place(slot, r, i):
        return (slot * REACH + r) * n_half + i

    def give_rows(side, c, start):
        packed = zero
        for slot in range(2):
            for r in range(REACH):
                for i in range(n_half):
                    at = place(slot, r, i)
                    rows_out[side, at] = work_row(slot, i, start + r).astype(BF16)
                    turn = lax.rem(edge_turn(c, start + r) + 2 + 4 * at, LANES)
                    packed = jnp.where(
                        group == at, pltpu.roll(edge_tile(slot, i, c), turn, 1), packed
                    )
        rows_out[side, 2 * REACH * n_half] = packed.astype(BF16)

    def take_rows(side, base):
        packed = rows_in[side, 2 * REACH * n_half].astype(F32)
        for slot in range(2):
            for r in range(REACH):

                def edge_of(i):
                    turn = (2 * LANES - 2 - 4 * place(slot, r, i)) % LANES
                    return pltpu.roll(packed, turn, 1)

                edge_total = edge_of(0)
                for i in range(1, n_half):
                    edge_total = edge_total + edge_of(i)
                prepare(
                    slot, base + r,
                    lambda i: rows_in[side, place(slot, r, i)].astype(F32),
                    edge_of, edge_total,
                )

    def lag_group(slot, row_at, count):
        @pl.loop(0, count)
        def _(n):
            r = row_at(n)
            sums = [None] * 25
            for i in range(n_half):
                centre = spread[slot, r + REACH, i, REACH]
                for k in range(25):
                    term = centre * spread[slot, r + k // 5, i, k % 5]
                    sums[k] = term if i == 0 else sums[k] + term
            for k in range(25):
                reduced[k, pl.ds(pl.multiple_of(n * 8, 8), 8), :] = sums[k]

    def lag_plane(k):
        total = reduced[k, pl.ds(0, CH, stride=8), :]
        for n in range(1, 8):
            total = total + reduced[k, pl.ds(n, CH, stride=8), :]
        return total * inverse

    def mean_rows(c):
        return pl.ds(pl.multiple_of(8 + c * CH, CH), CH)

    def put(value, g):
        return pltpu.roll(value, (4 * g + 2) % LANES, 1)

    def unput(value, g):
        return pltpu.roll(value, (2 * LANES - 4 * g - 2) % LANES, 1)

    def plain(c):
        start = c * CH + REACH
        return (lambda n: start + n), ((start, None),)

    def inner_ends():
        return (
            lambda n: jnp.where(n < 4, rows - CH + REACH + n, n - REACH),
            ((rows - CH + REACH, sub < 4), (-REACH, sub >= 4)),
        )

    def outer_ends():
        return (
            lambda n: lax.rem(rows - REACH + n, rows),
            ((rows - REACH, sub < 2), (-REACH, (sub >= 2) & (sub < 4))),
        )

    def last_rows():
        return (lambda n: CH - REACH + n), ((CH - REACH, sub < 4),)

    def layout(count, n_means, ends):
        side = 13 if count == CH else 7
        return side, side + 1, side + 1 + n_means, side + 1 + n_means + (3 if ends else 0)

    def send_group(m, row_at, chunk_means, count=CH, ends=False):
        at = 16 * m
        side_at, mean_at, low_at, length = layout(count, len(chunk_means), ends)
        lag_group(0, row_at, count)
        if count == CH:
            for p in range(13):
                sent[at + p] = lag_plane(12 + p)
        else:
            for p in range(0, 13, 2):
                pair = lag_plane(12 + p)
                if p < 12:
                    pair = jnp.where(sub < 4, pair, pltpu.roll(lag_plane(13 + p), 4, 0))
                sent[at + p // 2] = pair
        side, low = zero, [zero] * 3
        for k in range(12):
            if k % 5 == REACH and not ends:
                continue
            plane = lag_plane(k)
            if k % 5 != REACH:
                side = jnp.where(group == k, put(plane, k), side)
            if ends:
                turn = (2 * (k % 4) - 2) % 8
                low[k // 4] = jnp.where(
                    sub // 2 == k % 4, pltpu.roll(plane, turn, 0), low[k // 4]
                )
        for n, (mean, edge) in enumerate(chunk_means):
            sent[at + mean_at + n] = mean
            side = jnp.where(group == 12 + n, put(edge, 12 + n), side)
        sent[at + side_at] = side
        if ends:
            for n in range(3):
                sent[at + low_at + n] = low[n]
        to_partner(m, length).start()

    def chunk_mean(c):
        return tuple(means[0, kind, mean_rows(c), :] for kind in range(2))

    def add(k, at, value, keep=None):
        if keep is not None:
            value = jnp.where(keep, value, 0.0)
        totals[k, pl.ds(at, 8), :] += value

    def own_group(row_at, parts, count=CH):
        lag_group(1, row_at, count)
        for k in range(25):
            plane = lag_plane(k)
            for start, keep in parts:
                add(k, 8 + start, plane, keep)

    def add_far(m, base, keep, count, n_means, ends):
        at = 16 * m
        side_at, _, low_at, _ = layout(count, n_means, ends)
        gap = {}
        for a in range(-REACH, REACH + 1):
            value, edge = (
                means[1, kind, pl.ds(base + a, 8), :] - far_means[kind, pl.ds(base + a, 8), :]
                for kind in range(2)
            )
            for b in range(-REACH, REACH + 1):
                gap[a, b] = shifted(value, edge, b)
        centre = gap[0, 0] * 0.25
        side = got[at + side_at]
        for k in range(25):
            a, b = k // 5 - REACH, k % 5 - REACH
            value = centre * gap[a, b]
            if k >= 12:
                p = k - 12
                if count == CH:
                    plane = got[at + p]
                else:
                    plane = got[at + p // 2]
                    if p % 2:
                        plane = pltpu.roll(plane, 4, 0)
                value = value + plane
                if k > 12:
                    moved = pltpu.roll(plane, b % LANES, 1)
                    inside = (lane >= b) & (lane < LANES + b)
                    add(24 - k, base + a, jnp.where(inside, moved, 0.0), keep)
            else:
                direct = None
                if ends and a < 0:
                    direct = sub == 2 if a == -1 else (sub == 2) | (sub == 3)
                if b != 0:
                    outside = (lane < -b) | (lane >= LANES - b)
                    if direct is not None:
                        outside = outside & jnp.logical_not(direct)
                    value = value + jnp.where(outside, unput(side, k), 0.0)
                if direct is not None:
                    low = pltpu.roll(got[at + low_at + k // 4], (2 - 2 * (k % 4)) % 8, 0)
                    value = value + jnp.where(direct, low, 0.0)
            add(k, base, value, keep)

    def take_means(m, n, where):
        far_means[0, where, :] = got[16 * m + 14 + n]
        far_means[1, where, :] = unput(got[16 * m + 13], 12 + n)

    def take_group(m, parts, count=CH, n_means=1, ends=False):
        for start, keep in parts:
            add_far(m, 8 + start, keep, count, n_means, ends)

    def arrived(m, count, n_means, ends=False):
        to_partner(m, layout(count, n_means, ends)[3]).wait_recv()

    take_chunk(0)
    prepare_chunk(1, 0)
    give_rows(0, 0, 0)

    @pl.when(has_above)
    def _():
        row_copy(0, above).start()

    take_chunk(1)
    give_rows(1, chunks - 1, CH - REACH)

    @pl.when(has_below)
    def _():
        row_copy(1, below).start()

    send_group(0, inner_ends()[0], (chunk_mean(chunks - 1), chunk_mean(0)))
    prepare_chunk(1, chunks - 1)
    own_group(*inner_ends())

    last = chunks - 1
    wrap = last - 1

    @pl.loop(2, last)
    def _(step):
        c = chunk_at(step)
        take_chunk(step)
        send_group(step - 1, plain(c)[0], (chunk_mean(c),))
        prepare_chunk(1, c)
        own_group(*plain(c))

        @pl.when(step == 4)
        def _():
            empty = jnp.zeros((2, REACH, n_half, 5, 8, LANES), F32)

            @pl.when(has_below)
            def _():
                row_copy(0, below).wait_recv()
                take_rows(0, rows)

            @pl.when(jnp.logical_not(has_below))
            def _():
                spread[:, rows + REACH : rows + 2 * REACH] = empty

            @pl.when(has_above)
            def _():
                row_copy(1, above).wait_recv()
                take_rows(1, -REACH)

            @pl.when(jnp.logical_not(has_above))
            def _():
                spread[:, 0:REACH] = empty

            beyond = tuple(
                means[0, kind, pl.ds(0, 8), :] + means[0, kind, pl.ds(8 + rows, 8), :]
                for kind in range(2)
            )
            send_group(wrap, outer_ends()[0], (beyond,), count=4, ends=True)
            own_group(*outer_ends(), count=4)

    arrived(0, CH, 2)
    take_means(0, 0, mean_rows(chunks - 1))
    take_means(0, 1, mean_rows(0))
    take_group(0, inner_ends()[1], n_means=2)

    def take_step(step):
        c = chunk_at(step)
        arrived(step - 1, CH, 1)
        take_means(step - 1, 0, mean_rows(c))
        take_group(step - 1, plain(c)[1])

    @pl.loop(2, last - 1)
    def _(step):
        take_step(step)

    arrived(wrap, 4, 1, True)
    beyond = (got[16 * wrap + 8], unput(got[16 * wrap + 7], 12))
    for kind in range(2):
        far_means[kind, pl.ds(0, 8), :] = jnp.where(sub >= 8 - REACH, beyond[kind], 0.0)
        far_means[kind, pl.ds(8 + rows, 8), :] = jnp.where(sub < REACH, beyond[kind], 0.0)
    take_group(wrap, outer_ends()[1], count=4, ends=True)

    take_chunk(last)
    send_group(last, plain(1)[0], (chunk_mean(1),))
    send_group(last + 1, last_rows()[0], (), count=4)
    prepare_chunk(1, 1)
    own_group(*plain(1))
    own_group(*last_rows(), count=4)

    take_step(last - 1)
    arrived(last, CH, 1)
    take_means(last, 0, mean_rows(1))
    take_group(last, plain(1)[1])
    arrived(last + 1, 4, 0)
    take_group(last + 1, last_rows()[1], count=4, n_means=0)
    out[...] = totals[:, 8 : 8 + rows, :]

    all_of(block.at[:, :, pl.ds(0, n_half - 1)], send_sem, recv_sem.at[0]).wait_send()
    all_of(edges_in.at[:, pl.ds(0, n_half - 1)], edge_send, edge_recv).wait_send()
    length = (
        layout(CH, 2, False)[3] + (chunks - 2) * layout(CH, 1, False)[3]
        + layout(4, 1, True)[3] + layout(4, 0, False)[3]
    )
    every = sent.at[pl.ds(0, length)]
    all_of(every, part_send, part_recv.at[0]).wait_send()

    @pl.when(has_above)
    def _():
        row_copy(0, above).wait_send()

    @pl.when(has_below)
    def _():
        row_copy(1, below).wait_send()


def body(movie):
    frames, rows, width = movie.shape
    n_frame, n_strip = lax.axis_size("frame"), lax.axis_size("strip")
    chunks, n_half = rows // CH, n_frame // 2
    kernel = functools.partial(lag_kernel, n_frame, n_strip, 4, frames * n_frame)
    DMA = pltpu.SemaphoreType.DMA
    padded = rows + 16
    return pl.pallas_call(
        kernel,
        out_shape=jax.ShapeDtypeStruct((25, rows, width // n_frame), F32),
        in_specs=[pl.BlockSpec(memory_space=pl.ANY)],
        out_specs=pl.BlockSpec(memory_space=pltpu.VMEM),
        scratch_shapes=[
            pltpu.VMEM((chunks, 2, n_half, frames, CH, LANES), BF16),
            pltpu.VMEM((2, n_half, rows // 32, 8, LANES), BF16),
            pltpu.VMEM((n_frame, rows // 32, 8, LANES), BF16),
            pltpu.VMEM((2, 2 * REACH * n_half + 1, 8, LANES), BF16),
            pltpu.VMEM((2, 2 * REACH * n_half + 1, 8, LANES), BF16),
            pltpu.VMEM((frames, rows, width), BF16),
            pltpu.VMEM((2, rows + 2 * REACH, n_half, 5, 8, LANES), F32),
            pltpu.VMEM((frames * rows, LANES), F32),
            pltpu.VMEM((n_frame * CH * 8, LANES), F32),
            pltpu.VMEM((25, CH * 8, LANES), F32),
            pltpu.VMEM((16 * chunks + 16, 8, LANES), F32),
            pltpu.VMEM((16 * chunks + 16, 8, LANES), F32),
            pltpu.VMEM((2, 2, padded, LANES), F32),
            pltpu.VMEM((2, padded, LANES), F32),
            pltpu.VMEM((25, padded, LANES), F32),
            DMA, DMA((chunks,)), DMA, DMA, DMA, DMA, DMA((2,)), DMA((2,)),
            DMA, DMA((chunks + 1,)),
        ],
        compiler_params=pltpu.CompilerParams(
            collective_id=0, has_side_effects=True, vmem_limit_bytes=56 * 2**20
        ),
        name="lag_maps",
    )(movie)


def solution(mesh):
    return jax.shard_map(
        body,
        mesh=mesh,
        in_specs=(P("frame", "strip", None),),
        out_specs=P(None, "strip", "frame"),
        check_vma=False,
    )
```
